32 devices in a mesh: grp: 2 (over x), stn: 8 (over z, y), chan: 2 (over core).
Axes of the slice: x: 2, y: 2, z: 4, core: 2. Of those that a mesh axis runs over, the one named last changes fastest.
Arguments:
- voltage: bfloat16 [2, 32, 1048576], P(None, ('grp', 'stn'), 'chan'), parts along dimension 1, may hold values from -6 to 6
- earlier_samples: bfloat16 [2, 32, 61440], P(None, ('grp', 'stn')), parts along dimension 1, may hold values from -6 to 6
- prototype: float32 [16, 4096], replicated, may hold values from -1.5 to 1.5
Outputs:
- visibilities: float32 [2, 8192, 256], P(None, ('grp', 'stn', 'chan')), parts along dimension 1
The draws below stay inside these ranges and needn't reach their ends.
There are 2 independent parts, one for each index of `grp`. The reference program is written for one: setup_inputs(seed, part) draws one part's arguments, and reference() takes and returns one part's arrays. A program takes and returns all parts, laid end to end along the dimension named above; an argument that names none is the same for every part. Nothing has to cross between parts.
All inputs are finite; a program needn't handle non-finite values.
Results may differ from the reference program's by a relative error of at most 0.0044.
Values may be sent and summed in bfloat16 or wider, within the bound.
No kernel may reach another device: no remote copies, remote signals or barrier semaphores. Data moves between devices by JAX's collectives and lax.ppermute only.
A program may use at most 64 MiB of HBM per device.

```python
import math
import jax
import jax.numpy as jnp
from jax import lax

NCH = 4096
FA = 64
FB = 64
TAPS = 16
INPUTS = 16
SPEC = 256


def shard_levels(own_key, extent, cuts, smallest, largest):
    loudness, own = 1.0, jax.random.fold_in(own_key, 6)
    for position, parts in cuts:
        steps = jnp.exp(jax.random.uniform(jax.random.fold_in(own, position), (parts,), jnp.float32, smallest / len(cuts), largest / len(cuts)))
        loudness = loudness * jnp.repeat(steps, extent[position] // parts).reshape([-1 if axis == position else 1 for axis in range(len(extent))])
    return loudness


def bell_draw(rng, extent, width, limit, pieces=(), dtype=jnp.bfloat16):
    drawn = jax.random.normal(rng, extent, jnp.float32) * width
    if len(pieces) > 0:
        drawn = shard_levels(rng, extent, pieces, -0.22, 0.18) * drawn
    return jnp.clip(drawn, min=-limit, max=limit).astype(dtype)


def setup_inputs(seed: int = 0, part: int = 0) -> dict:
    key_of = jax.random.split(jax.random.key(seed), 4)
    own_keys = jax.random.split(jax.random.fold_in(key_of[3], part), 4)
    voltage = bell_draw(own_keys[0], (2, INPUTS, SPEC * NCH), 1.0, 6.0, ((1, 8), (2, 2)))
    earlier_samples = bell_draw(own_keys[1], (2, INPUTS, (TAPS - 1) * NCH), 1.0, 6.0, ((1, 8),))
    prototype = bell_draw(key_of[2], (TAPS, NCH), TAPS ** -0.5, 1.5, (), jnp.float32)
    return {"voltage": voltage, "earlier_samples": earlier_samples, "prototype": prototype}


def small_tables(length):
    row_index = lax.broadcasted_iota(jnp.int32, (length, length), 0)
    col_index = lax.broadcasted_iota(jnp.int32, (length, length), 1)
    phase_angle = ((row_index * col_index) % length).astype(jnp.float32) * (2.0 * math.pi / length)
    return jnp.cos(phase_angle).astype(jnp.bfloat16), jnp.sin(phase_angle).astype(jnp.bfloat16)


def reference(voltage, earlier_samples, prototype):
    stream = jnp.concatenate([earlier_samples, voltage], axis=2).astype(jnp.float32)
    frames = stream.reshape(2, INPUTS, SPEC + TAPS - 1, NCH)
    filtered = jnp.zeros((2, INPUTS, SPEC, NCH), jnp.float32)
    for tap_number in range(TAPS):
        filtered = filtered + prototype[tap_number].astype(jnp.float32) * frames[:, :, tap_number:tap_number + SPEC]
    rounded = lax.optimization_barrier(filtered.astype(jnp.bfloat16))
    factored = rounded.astype(jnp.float32).reshape(2, INPUTS * SPEC, FA, FB)
    first_cos, first_sin = small_tables(FA)
    second_cos, second_sin = small_tables(FB)
    high = lax.Precision.HIGHEST
    with_cos = jnp.einsum("crab,ak->crkb", factored, first_cos.astype(jnp.float32), precision=high)
    with_sin = jnp.einsum("crab,ak->crkb", factored, first_sin.astype(jnp.float32), precision=high)
    g_real = with_cos[0] + with_sin[1]
    g_imag = with_cos[1] - with_sin[0]
    row_k = lax.broadcasted_iota(jnp.int32, (FA, FB), 0)
    col_b = lax.broadcasted_iota(jnp.int32, (FA, FB), 1)
    twist = ((row_k * col_b) % NCH).astype(jnp.float32) * (2.0 * math.pi / NCH)
    twist_cos = jnp.cos(twist)
    twist_sin = jnp.sin(twist)
    inner = jnp.stack([g_real * twist_cos + g_imag * twist_sin, g_imag * twist_cos - g_real * twist_sin])
    inner = lax.optimization_barrier(inner.astype(jnp.bfloat16)).astype(jnp.float32)
    second_a = jnp.einsum("crkb,bm->crkm", inner, second_cos.astype(jnp.float32), precision=high)
    second_b = jnp.einsum("crkb,bm->crkm", inner, second_sin.astype(jnp.float32), precision=high)
    scale_factor = NCH ** -0.5
    real_part = (second_a[0] + second_b[1]) * scale_factor
    imag_part = (second_a[1] - second_b[0]) * scale_factor
    ordered = jnp.transpose(jnp.stack([real_part, imag_part]), (0, 1, 3, 2))
    spectra = ordered.astype(jnp.bfloat16).reshape(2, INPUTS, SPEC, NCH)
    block_size = math.gcd(NCH, 512)
    channel_major = jnp.moveaxis(spectra.reshape(2, INPUTS, SPEC, NCH // block_size, block_size), 3, 0)

    def correlate(panel):
        wide = panel.astype(jnp.float32)
        products = jnp.einsum("xisc,yjsc->xycij", wide, wide, precision=high)
        real_sum = products[0, 0] + products[1, 1]
        imag_sum = products[1, 0] - products[0, 1]
        return jnp.stack([real_sum, imag_sum]) / SPEC

    blocks = lax.map(correlate, channel_major)
    return jnp.transpose(blocks, (1, 0, 2, 3, 4)).reshape(2, NCH, INPUTS * INPUTS)
```

```python
import functools

import jax
import jax.numpy as jnp
import numpy as np
from jax import lax
from jax.experimental import pallas as pl
from jax.experimental.pallas import tpu as pltpu
from jax.sharding import PartitionSpec as P

FA = 64
LANES = 128
STEP = 8
SHARES = (4, 8, 4)
F32 = jnp.float32
BF16 = jnp.bfloat16
ANY = pl.BlockSpec(memory_space=pl.ANY)
VMEM = pl.BlockSpec(memory_space=pltpu.VMEM)
SMEM = pl.BlockSpec(memory_space=pltpu.SMEM)


def cos_sin(index, length):
    angle = (index % length).astype(np.float32) * np.float32(2.0 * np.pi / length)
    return np.cos(angle), np.sin(angle)


def small_tables(length):
    cos, sin = cos_sin(np.outer(np.arange(length), np.arange(length)), length)
    return cos.astype(BF16).astype(np.float32), sin.astype(BF16).astype(np.float32)


def rotation(cos, sin):
    return np.stack([np.stack([cos, sin]), np.stack([-sin, cos])])


def first_table():
    turn = rotation(*small_tables(FA))
    turn = turn.reshape(2, 2, FA // 2, 2, FA)
    table = np.einsum("dchlk,ef->edklchf", turn, np.eye(2))
    return table.reshape(4 * FA, 4 * FA).astype(BF16)


def second_table(length, stations):
    turn = rotation(*small_tables(length)) * (FA * length) ** -0.5
    turn = turn.reshape(2, 2, length, stations, length // stations)
    table = np.einsum("dcbnm,st->nsdmctb", turn, np.eye(2))
    return table.reshape(4 * length, 4 * length).astype(BF16)


def twist_tables(length):
    cos, sin = cos_sin(np.outer(np.arange(FA), np.arange(length)), FA * length)
    return np.stack([np.tile(cos, (1, 2)), np.tile(sin, (1, 2))]).astype(np.float32)


def rows_dot(left, right, axis):
    return lax.dot_general(left, right, (((1,), (axis,)), ((), ())), preferred_element_type=F32)


def spectra_kernel(first, count, taps, stations, place, *refs):
    samples, earlier, passed, taps_ref, first_ref, twist_ref, second_ref = refs[:7]
    outs = refs[7 : 7 + stations]
    frames, mixed, inner, second, sems = refs[7 + stations :]
    per = 2 * FA // 2
    held = (taps - 1) * per
    copies = []
    if first >= taps - 1:
        for comp in range(2):
            copies.append(
                pltpu.make_async_copy(
                    samples.at[comp, pl.ds(first * per - held, held + count * per)],
                    frames.at[comp],
                    sems.at[comp],
                )
            )
            copies[-1].start()
    else:
        for comp in range(2):
            copies.append(
                pltpu.make_async_copy(
                    samples.at[comp, pl.ds(0, count * per)],
                    frames.at[comp, pl.ds(held, count * per)],
                    sems.at[comp],
                )
            )
            copies[-1].start()

        @pl.when(place[1] == 0)
        def _():
            pltpu.make_async_copy(earlier, frames.at[:, pl.ds(0, held)], sems.at[2]).start()

        @pl.when(place[1] != 0)
        def _():
            pltpu.make_async_copy(passed, frames.at[:, pl.ds(0, held)], sems.at[2]).start()

        copies.append(pltpu.make_async_copy(earlier, frames.at[:, pl.ds(0, held)], sems.at[2]))
    share = second_ref.shape[0] // stations
    for offset in range(stations):
        owner = place[0] ^ offset
        start = pl.multiple_of(owner * share, share)
        second[offset * share : (offset + 1) * share] = second_ref[pl.ds(start, share)]
    for copy in copies:
        copy.wait()
    low_half = lax.broadcasted_iota(jnp.int32, (16, LANES), 1) < LANES // 2

    def block(index, carry):
        base = index * (STEP * per)
        for comp in range(2):
            for quarter in range(per // 16):
                row = quarter * 16
                window = []
                for step in range(taps - 1 + STEP):
                    start = pl.multiple_of(base + step * per + row, 16)
                    window.append(frames[comp, pl.ds(start, 16)].astype(F32))
                sums = None
                for tap in range(taps):
                    weight = taps_ref[tap, row : row + 16]
                    terms = [weight * window[tap + step] for step in range(STEP)]
                    sums = terms if sums is None else [x + y for x, y in zip(sums, terms)]
                for pair in range(STEP // 2):
                    even, odd = sums[2 * pair], sums[2 * pair + 1]
                    low = jnp.where(low_half, even, pltpu.roll(odd, LANES // 2, 1))
                    high = jnp.where(low_half, pltpu.roll(even, LANES // 2, 1), odd)
                    lane = (pair % 2) * LANES
                    at = comp * per + row
                    mixed[pair // 2, at : at + 16, lane : lane + LANES] = low.astype(BF16)
                    at = at + 2 * per
                    mixed[pair // 2, at : at + 16, lane : lane + LANES] = high.astype(BF16)
        for half in range(STEP // 4):
            g = rows_dot(first_ref[...], mixed[half], 0)
            for pair in range(2):
                for member in range(2):
                    lane = pair * LANES
                    g_re = g[2 * member * FA : (2 * member + 1) * FA, lane : lane + LANES]
                    g_im = g[(2 * member + 1) * FA : (2 * member + 2) * FA, lane : lane + LANES]
                    cos, sin = twist_ref[0], twist_ref[1]
                    at = (2 * pair + member) * FA
                    inner[half, at : at + FA, :LANES] = (g_re * cos + g_im * sin).astype(BF16)
                    inner[half, at : at + FA, LANES:] = (g_im * cos - g_re * sin).astype(BF16)
            spectra = rows_dot(second[...], inner[half], 1).astype(BF16)
            for pair in range(2):
                for offset in range(stations):
                    outs[offset][index * (STEP // 2) + 2 * half + pair] = spectra[
                        offset * share : (offset + 1) * share, pair * LANES : (pair + 1) * LANES
                    ]
        return carry

    lax.fori_loop(0, count // STEP, block, 0)


def spectra_of(first, count, place, samples, earlier, passed, taps_table, stations, length):
    taps = taps_table.shape[0]
    share = 4 * length // stations
    rows = (taps - 1 + count) * FA
    tables = (first_table(), twist_tables(length), second_table(length, stations))
    return pl.pallas_call(
        functools.partial(spectra_kernel, first, count, taps, stations),
        out_shape=[jax.ShapeDtypeStruct((count // 2, share, LANES), BF16)] * stations,
        in_specs=[SMEM, ANY, ANY, ANY, VMEM, VMEM, VMEM, VMEM],
        out_specs=[VMEM] * stations,
        scratch_shapes=[
            pltpu.VMEM((2, rows, LANES), BF16),
            pltpu.VMEM((STEP // 4, 4 * FA, 2 * LANES), BF16),
            pltpu.VMEM((STEP // 4, 4 * FA, 2 * LANES), BF16),
            pltpu.VMEM((4 * length, 4 * FA), BF16),
            pltpu.SemaphoreType.DMA((3,)),
        ],
        cost_estimate=pl.CostEstimate(
            flops=count * 8 * 10**6, bytes_accessed=count * 65536, transcendentals=0
        ),
        name=f"spectra_{first}",
    )(place, samples, earlier, passed, taps_table, *tables)


def pair_rows(stations):
    pairs = [(a, b) for a in range(stations) for b in range(a, stations)]
    return {pair: 2 * row for row, pair in enumerate(pairs)}


def products_kernel(stations, carried, *refs):
    blocks = refs[:stations]
    before = refs[stations] if carried else None
    out = refs[-1]
    rows = pair_rows(stations)
    span = blocks[0].shape[1] // 4

    def load(block, step, low):
        both = block[step, low * 2 * span : (low + 1) * 2 * span].astype(F32)
        return both[:span], both[span:]

    for left in range(0, stations, 2):
        for right in range(left, stations, 2):
            members = [(a, b) for a in (left, left + 1) for b in (right, right + 1) if a <= b]

            def body(step, sums):
                for low in range(2):
                    a_side = {a: load(blocks[a], step, low) for a in (left, left + 1)}
                    b_side = a_side
                    if right != left:
                        b_side = {b: load(blocks[b], step, low) for b in (right, right + 1)}
                    turned = {
                        b: [pltpu.roll(x, LANES // 2, 1) for x in b_side[b]] for b in b_side
                    }
                    new = []
                    for a, b in members:
                        a_re, a_im = a_side[a]
                        for b_re, b_im in (b_side[b], turned[b]):
                            new.append(a_re * b_re + a_im * b_im)
                            new.append(a_im * b_re - a_re * b_im)
                    sums = [x + y for x, y in zip(sums, new)]
                return sums

            start = []
            for pair in members:
                for variant in range(2):
                    for comp in range(2):
                        at = (rows[pair] + variant) * span
                        if carried:
                            start.append(before[comp, at : at + span])
                        else:
                            start.append(jnp.zeros((span, LANES), F32))
            sums = lax.fori_loop(0, blocks[0].shape[0], body, start, unroll=2)
            place = iter(sums)
            for pair in members:
                for variant in range(2):
                    for comp in range(2):
                        at = (rows[pair] + variant) * span
                        out[comp, at : at + span] = next(place)


def products_of(blocks, before):
    stations = len(blocks)
    count = len(pair_rows(stations)) * 2
    span = blocks[0].shape[1] // 4
    carried = before is not None
    arrays = list(blocks) + ([before] if carried else [])
    steps = 2 * blocks[0].shape[0]
    return pl.pallas_call(
        functools.partial(products_kernel, stations, carried),
        out_shape=jax.ShapeDtypeStruct((2, count * span, LANES), F32),
        in_specs=[VMEM] * len(arrays),
        out_specs=VMEM,
        cost_estimate=pl.CostEstimate(
            flops=steps * 4 * 10**6, bytes_accessed=steps * 65536, transcendentals=0
        ),
        name="products",
    )(*arrays)


def visibility_kernel(stations, total, place, own, other, out):
    span = 2 * (own.shape[1] // (4 * len(pair_rows(stations))))
    count = own.shape[1] // span
    mine = span // 2
    width = 4 * stations * stations
    me = place[0]
    row = lax.broadcasted_iota(jnp.int32, (count, width), 0)
    col = lax.broadcasted_iota(jnp.int32, (count, width), 1)
    variant = row % 2
    pair = row // 2
    a_rel = jnp.zeros_like(row)
    b_rel = jnp.zeros_like(row)
    for (a, b), at in pair_rows(stations).items():
        a_rel = jnp.where(pair == at // 2, a, a_rel)
        b_rel = jnp.where(pair == at // 2, b, b_rel)
    a_at = a_rel ^ me
    b_at = b_rel ^ me
    picks = []
    for member in range(2):
        i_at = 2 * a_at + member
        j_at = 2 * b_at + (variant ^ member)
        plain = col == i_at * (2 * stations) + j_at
        mirror = (col == j_at * (2 * stations) + i_at) & (a_rel != b_rel)
        for sign in (1.0, -1.0):
            picks.append(jnp.where(plain, 1.0, jnp.where(mirror, sign, 0.0)))
    for low in range(mine):
        start = place[1] * mine + low
        for comp in range(2):
            lanes = (
                own[comp, pl.ds(start, count, stride=span)]
                + other[comp, pl.ds(start, count, stride=span)]
            ) * (1.0 / total)
            turned = lanes.T
            value = None
            for member in range(2):
                part = lax.dot_general(
                    turned[member * FA : (member + 1) * FA],
                    picks[2 * member + comp],
                    (((1,), (0,)), ((), ())),
                    precision=lax.Precision.HIGHEST,
                    preferred_element_type=F32,
                )
                value = part if value is None else value + part
            out[comp, low * FA : (low + 1) * FA] = value


def shards(voltage, earlier_samples, prototype):
    components, local_inputs, samples = voltage.shape
    tap_count, channels = prototype.shape
    spectra_here = samples // channels
    length = channels // FA
    stations = lax.axis_size("stn")
    cores = lax.axis_size("chan")
    per = channels // LANES

    def by_tile(block):
        tiles = block.reshape(components, local_inputs, -1, LANES)
        return jnp.transpose(tiles, (0, 2, 1, 3)).reshape(components, -1, LANES)

    stream = by_tile(voltage)
    earlier = by_tile(earlier_samples)
    tail = stream[:, stream.shape[1] - earlier.shape[1] :]
    passed = lax.ppermute(tail, "chan", [(i, i + 1) for i in range(cores - 1)])
    taps_table = jnp.repeat(prototype.reshape(tap_count, per, 1, LANES), 2, axis=2)
    taps_table = taps_table.reshape(tap_count, 2 * per, LANES)
    place = jnp.stack([lax.axis_index("stn"), lax.axis_index("chan")]).astype(jnp.int32)
    whole = sum(SHARES)
    first = spectra_here
    sums = None
    chunks = []
    for share in SHARES:
        count = spectra_here * share // whole
        first -= count
        chunks.append(
            spectra_of(
                first, count, place, stream, earlier, passed, taps_table, stations, length
            )
        )
    order = sorted(range(1, stations), key=lambda d: (d < 4, d))
    total = spectra_here * cores
    if 2 * length // stations == 16:
        for blocks in chunks:
            blocks = list(blocks)
            for offset in order:
                route = [(i, i ^ offset) for i in range(stations)]
                blocks[offset] = lax.ppermute(blocks[offset], "stn", route)
            sums = products_of(blocks, sums)
        other = lax.ppermute(sums, "chan", [(i, i ^ 1) for i in range(cores)])
        owned = channels // (stations * cores)
        return pl.pallas_call(
            functools.partial(visibility_kernel, stations, total),
            out_shape=jax.ShapeDtypeStruct((2, owned, 4 * stations * stations), F32),
            in_specs=[SMEM, VMEM, VMEM],
            out_specs=VMEM,
            name="visibility",
        )(place, sums, other)
    joined = [jnp.concatenate([blocks[d] for blocks in chunks]) for d in range(stations)]
    joined = jnp.stack(joined)
    me = lax.axis_index("stn")
    joined = joined[jnp.arange(stations) ^ me]
    span = length // stations // cores
    joined = joined.reshape(stations, spectra_here // 2, 2, 2, cores, span, 2, FA)
    joined = jnp.transpose(joined, (3, 6, 1, 2, 0, 4, 5, 7))
    joined = joined.reshape(2, 2, spectra_here, stations * cores, span * FA)
    moved = lax.all_to_all(joined, ("stn", "chan"), split_axis=3, concat_axis=3, tiled=True)
    moved = moved.reshape(2, 2, spectra_here, stations, cores, span * FA)
    moved = jnp.transpose(moved, (0, 3, 1, 4, 2, 5))
    moved = moved.reshape(2, 2 * stations, total, span * FA)
    products = jnp.einsum("xisc,yjsc->xycij", moved, moved, preferred_element_type=F32)
    real_sum = products[0, 0] + products[1, 1]
    imag_sum = products[1, 0] - products[0, 1]
    averaged = jnp.stack([real_sum, imag_sum]) / total
    return averaged.reshape(2, span * FA, 4 * stations * stations)


def solution(mesh):
    in_specs = (P(None, ("grp", "stn"), "chan"), P(None, ("grp", "stn"), None), P())
    out_specs = P(None, ("grp", "stn", "chan"), None)
    return jax.shard_map(shards, mesh=mesh, in_specs=in_specs, out_specs=out_specs, check_vma=False)
```

```python
import functools

import jax
import jax.numpy as jnp
import numpy as np
from jax import lax
from jax.experimental import pallas as pl
from jax.experimental.pallas import tpu as pltpu
from jax.sharding import PartitionSpec as P


FA = 64
LANES = 128
STEP = 8
SHARES = (4, 8, 4)
F32 = jnp.float32
BF16 = jnp.bfloat16
ANY = pl.BlockSpec(memory_space=pl.ANY)
VMEM = pl.BlockSpec(memory_space=pltpu.VMEM)


def cos_sin(index, length):
    angle = (index % length).astype(np.float32) * np.float32(2.0 * np.pi / length)
    return np.cos(angle), np.sin(angle)


def small_tables(length):
    cos, sin = cos_sin(np.outer(np.arange(length), np.arange(length)), length)
    return cos.astype(BF16).astype(np.float32), sin.astype(BF16).astype(np.float32)


def rotation(cos, sin):
    return np.stack([np.stack([cos, sin]), np.stack([-sin, cos])])


def first_table():
    turn = rotation(*small_tables(FA))
    turn = turn.reshape(2, 2, FA // 2, 2, FA)
    table = np.einsum("dchlk,ef->edklchf", turn, np.eye(2))
    return table.reshape(4 * FA, 4 * FA).astype(BF16)


def second_table(length, stations):
    turn = rotation(*small_tables(length)) * (FA * length) ** -0.5
    turn = turn.reshape(2, 2, length, stations, length // stations)
    table = np.einsum("dcbnm,st->nsdmctb", turn, np.eye(2))
    return table.reshape(4 * length, 4 * length).astype(BF16)


def twist_tables(length):
    cos, sin = cos_sin(np.outer(np.arange(FA), np.arange(length)), FA * length)
    return np.stack([np.tile(cos, (1, 2)), np.tile(sin, (1, 2))]).astype(np.float32)


def rows_dot(left, right, axis):
    return lax.dot_general(left, right, (((1,), (axis,)), ((), ())), preferred_element_type=F32)


def spectra_kernel(first, count, taps, stations, last, *refs):
    samples, earlier, passed, prototype, first_hbm, twist_hbm, second_hbm, _ = refs[:8]
    outs = refs[8 : 8 + stations]
    refs = refs[8 + stations :]
    tail = None
    if last:
        tail, refs = refs[0], refs[1:]
    frames, wide, filtered, proto, weights, first_ref, twist_ref, second_in, second, sems = refs
    per = FA
    held = (taps - 1) * per
    total = held + count * per
    tables = [
        pltpu.make_async_copy(source, target, sems.at[at])
        for at, (source, target) in enumerate(
            ((first_hbm, first_ref), (twist_hbm, twist_ref), (second_hbm, second_in))
        )
    ]
    proto_copy = pltpu.make_async_copy(prototype, proto, sems.at[3])
    proto_copy.start()
    lead = 0 if first >= taps - 1 else held
    copies = [
        pltpu.make_async_copy(
            samples.at[comp, pl.ds(first * per - held + lead, total - lead)],
            frames.at[comp, pl.ds(lead, total - lead)],
            sems.at[4 + comp],
        )
        for comp in range(2)
    ]
    for copy in copies + tables:
        copy.start()
    if lead:
        chan = lax.axis_index("chan")
        history = frames.at[:, pl.ds(0, held)]

        @pl.when(chan == 0)
        def _():
            pltpu.make_async_copy(earlier, history, sems.at[6]).start()

        @pl.when(chan != 0)
        def _():
            pltpu.make_async_copy(passed, history, sems.at[6]).start()

        copies.append(pltpu.make_async_copy(earlier, history, sems.at[6]))
    proto_copy.wait()
    for high in range(per // 2):
        for group in range(taps // 8):
            lane = high * LANES
            rows = proto[group * 8 : (group + 1) * 8, lane : lane + LANES]
            for member in range(2):
                at = group * 8 * per + 2 * high + member
                weights[pl.ds(at, 8, stride=per)] = rows
    for copy in copies:
        copy.wait()
    if last:
        tail_copy = pltpu.make_async_copy(
            frames.at[:, pl.ds(count * per, held)], tail, sems.at[6]
        )
        tail_copy.start()

    def widen(frame, carry):
        at = pl.multiple_of(frame * per, per)
        for comp in range(2):
            wide[comp, pl.ds(at, per)] = frames[comp, pl.ds(at, per)].astype(F32)
        return carry

    lax.fori_loop(0, total // per, widen, 0)

    def strip(index, carry):
        comp = index // (per // 16)
        row = (index % (per // 16)) * 16

        def run(block, carry):
            window = []
            for step in range(taps - 1 + STEP):
                at = pl.multiple_of((block * STEP + step) * per + row, 16)
                window.append(wide[comp, pl.ds(at, 16)])
            sums = None
            for tap in range(taps):
                weight = weights[pl.ds(pl.multiple_of(tap * per + row, 16), 16)]
                terms = [weight * window[tap + step] for step in range(STEP)]
                sums = terms if sums is None else [x + y for x, y in zip(sums, terms)]
            for step in range(STEP):
                at = pl.multiple_of(comp * per + row, 16)
                filtered[block * STEP + step, pl.ds(at, 16)] = sums[step].astype(BF16)
            return carry

        return lax.fori_loop(0, count // STEP, run, carry)

    lax.fori_loop(0, 2 * per // 16, strip, 0)
    for copy in tables:
        copy.wait()
    share = second_in.shape[0] // stations
    me = lax.axis_index("stn")
    for offset in range(stations):
        start = pl.multiple_of((me ^ offset) * share, share)
        second[offset * share : (offset + 1) * share] = second_in[pl.ds(start, share)]
    low_half = lax.broadcasted_iota(jnp.int32, (2 * per, LANES), 1) < LANES // 2

    def transform(index, carry):
        mixed = []
        for pair in range(2):
            even = filtered[index * 4 + 2 * pair].astype(F32)
            odd = filtered[index * 4 + 2 * pair + 1].astype(F32)
            low = jnp.where(low_half, even, pltpu.roll(odd, LANES // 2, 1))
            high = jnp.where(low_half, pltpu.roll(even, LANES // 2, 1), odd)
            mixed.append(jnp.concatenate([low.astype(BF16), high.astype(BF16)], axis=0))
        g = rows_dot(first_ref[...], jnp.concatenate(mixed, axis=1), 0)
        cos, sin = twist_ref[0], twist_ref[1]
        inner = []
        for member in range(2):
            for pair in range(2):
                lane = pair * LANES
                g_re = g[2 * member * FA : (2 * member + 1) * FA, lane : lane + LANES]
                g_im = g[(2 * member + 1) * FA : (2 * member + 2) * FA, lane : lane + LANES]
                inner_re = (g_re * cos + g_im * sin).astype(BF16)
                inner_im = (g_im * cos - g_re * sin).astype(BF16)
                inner.append(jnp.concatenate([inner_re, inner_im], axis=1))
        spectra = rows_dot(second[...], jnp.concatenate(inner, axis=0), 1).astype(BF16)
        for member in range(2):
            lane = member * LANES
            for offset in range(stations):
                row = offset * share
                outs[offset][index, member] = spectra[row : row + share, lane : lane + LANES]
        return carry

    lax.fori_loop(0, count // 4, transform, 0, unroll=2)
    if last:
        tail_copy.wait()


def spectra_of(first, count, samples, earlier, passed, prototype, after, stations, last):
    taps, channels = prototype.shape
    length = channels // FA
    share = 4 * length // stations
    held = (taps - 1) * FA
    rows = held + count * FA
    tables = (first_table(), twist_tables(length), second_table(length, stations))
    out_shape = [jax.ShapeDtypeStruct((count // 4, 2, share, LANES), BF16)] * stations
    if last:
        out_shape.append(jax.ShapeDtypeStruct((2, held, LANES), BF16))
    return pl.pallas_call(
        functools.partial(spectra_kernel, first, count, taps, stations, last),
        out_shape=out_shape,
        in_specs=[ANY] * 8,
        out_specs=[VMEM] * stations + [ANY] * last,
        scratch_shapes=[
            pltpu.VMEM((2, rows, LANES), BF16),
            pltpu.VMEM((2, rows, LANES), F32),
            pltpu.VMEM((count, 2 * FA, LANES), BF16),
            pltpu.VMEM((taps, channels), F32),
            pltpu.VMEM((taps * FA, LANES), F32),
            pltpu.VMEM((4 * FA, 4 * FA), BF16),
            pltpu.VMEM((2, FA, LANES), F32),
            pltpu.VMEM((4 * length, 4 * length), BF16),
            pltpu.VMEM((4 * length, 4 * length), BF16),
            pltpu.SemaphoreType.DMA((7,)),
        ],
        cost_estimate=pl.CostEstimate(
            flops=count * 8 * 10**6, bytes_accessed=count * 65536, transcendentals=0
        ),
    )(samples, earlier, passed, prototype, *tables, after)


def pair_rows(inputs):
    pairs = [(a, b) for a in range(inputs) for b in range(a, inputs)]
    return {pair: row for row, pair in enumerate(pairs)}


def products_kernel(stations, carried, fold, *refs):
    blocks = refs[:stations]
    before = refs[stations] if carried else None
    out = refs[-1]
    rows = pair_rows(2 * stations)
    span = blocks[0].shape[2] // 4
    group = 4

    def load(member, step, low):
        tile = blocks[member // 2][step, member % 2, low * 2 * span : (low + 1) * 2 * span]
        both = tile.astype(F32)
        return both[:span], both[span:]

    for left in range(0, 2 * stations, group):
        for right in range(left, 2 * stations, group):
            a_list = range(left, left + group)
            b_list = range(right, right + group)
            members = [(a, b) for a in a_list for b in b_list if a <= b]
            wanted = [(a, b, comp) for a, b in members for comp in range(2) if a != b or comp == 0]

            def body(step, sums):
                for low in range(2):
                    a_side = {a: load(a, step, low) for a in a_list}
                    b_side = a_side
                    if right != left:
                        b_side = {b: load(b, step, low) for b in b_list}
                    new = []
                    for total, (a, b, comp) in zip(sums, wanted):
                        a_re, a_im = a_side[a]
                        b_re, b_im = b_side[b]
                        if comp == 0:
                            new.append(total + a_re * b_re + a_im * b_im)
                        else:
                            new.append(total + a_im * b_re - a_re * b_im)
                    sums = new
                return sums

            start = []
            for a, b, comp in wanted:
                at = (2 * rows[a, b] + comp) * span
                if carried:
                    start.append(before[at : at + span])
                else:
                    start.append(jnp.zeros((span, LANES), F32))
            sums = lax.fori_loop(0, blocks[0].shape[0], body, start)
            sums = dict(zip(wanted, sums))
            for a, b in members:
                re = sums[a, b, 0]
                im = sums.get((a, b, 1), jnp.zeros_like(re))
                at = rows[a, b] * span
                if fold:
                    low_half = lax.broadcasted_iota(jnp.int32, re.shape, 1) < LANES // 2
                    re = re + pltpu.roll(re, LANES // 2, 1)
                    im = im + pltpu.roll(im, LANES // 2, 1)
                    out[at : at + span] = jnp.where(low_half, re, im)
                else:
                    out[2 * at : 2 * at + span] = re
                    out[2 * at + span : 2 * at + 2 * span] = im


def products_of(blocks, before, fold):
    stations = len(blocks)
    count = len(pair_rows(2 * stations)) * (1 if fold else 2)
    span = blocks[0].shape[2] // 4
    carried = before is not None
    arrays = list(blocks) + ([before] if carried else [])
    steps = 4 * blocks[0].shape[0]
    return pl.pallas_call(
        functools.partial(products_kernel, stations, carried, fold),
        out_shape=jax.ShapeDtypeStruct((count * span, LANES), F32),
        in_specs=[VMEM] * len(arrays),
        out_specs=VMEM,
        cost_estimate=pl.CostEstimate(
            flops=steps * 4 * 10**6, bytes_accessed=steps * 65536, transcendentals=0
        ),
        name="products",
    )(*arrays)


def visibility_kernel(stations, total, own, other, out):
    inputs = 2 * stations
    rows = pair_rows(inputs)
    count = len(rows)
    span = own.shape[0] // count
    mine = span // 2
    width = inputs * inputs
    turn = 2 * lax.axis_index("stn")
    row = lax.broadcasted_iota(jnp.int32, (count, width), 0)
    col = lax.broadcasted_iota(jnp.int32, (count, width), 1)
    i_rel = jnp.zeros_like(row)
    for a in range(1, inputs):
        i_rel = i_rel + (row >= rows[a, a]).astype(jnp.int32)
    j_rel = row - (i_rel * inputs - i_rel * (i_rel - 1) // 2) + i_rel
    i_at, j_at = i_rel ^ turn, j_rel ^ turn
    plain = col == i_at * inputs + j_at
    mirror = col == j_at * inputs + i_at
    picks = [
        jnp.where(plain, 1.0, jnp.where(mirror, sign, 0.0)).astype(BF16) for sign in (1.0, -1.0)
    ]
    core = lax.axis_index("chan")
    for low in range(mine):
        at = pl.ds(core * mine + low, count, stride=span)
        lanes = ((own[at] + other[at]) * (1.0 / total)).T
        for comp in range(2):
            rest = lanes[comp * FA : (comp + 1) * FA]
            value = None
            for _ in range(3):
                piece = rest.astype(BF16)
                part = rows_dot(piece, picks[comp], 0)
                value = part if value is None else value + part
                rest = rest - piece.astype(F32)
            out[comp, low * FA : (low + 1) * FA] = value


def send_order(stations):
    return sorted(range(1, stations), key=lambda d: (d < stations // 2, d))


def shards(voltage, earlier_samples, prototype):
    components, local_inputs, samples = voltage.shape
    _, channels = prototype.shape
    spectra_here = samples // channels
    length = channels // FA
    stations = lax.axis_size("stn")
    cores = lax.axis_size("chan")
    total = spectra_here * cores

    def by_tile(block):
        tiles = block.reshape(components, local_inputs, -1, LANES)
        return jnp.transpose(tiles, (0, 2, 1, 3)).reshape(components, -1, LANES)

    stream = by_tile(voltage)
    earlier = by_tile(earlier_samples)
    whole = sum(SHARES)
    first = spectra_here
    chunks = []
    passed, after = earlier, earlier
    for chunk, share in enumerate(SHARES):
        count = spectra_here * share // whole
        first -= count
        history = earlier if first else passed
        blocks = list(
            spectra_of(
                first, count, stream, earlier, history, prototype, after, stations, chunk == 0
            )
        )
        if chunk == 0:
            route = [(i, i + 1) for i in range(cores - 1)]
            passed = lax.ppermute(blocks.pop(), "chan", route)
        after = blocks[0]
        chunks.append(blocks)
    if 2 * length // stations == 16:
        sums = None
        for chunk, blocks in enumerate(chunks):
            for offset in send_order(stations):
                route = [(i, i ^ offset) for i in range(stations)]
                blocks[offset] = lax.ppermute(blocks[offset], "stn", route)
            sums = products_of(blocks, sums, chunk == len(chunks) - 1)
        other = lax.ppermute(sums, "chan", [(i, i ^ 1) for i in range(cores)])
        owned = channels // (stations * cores)
        return pl.pallas_call(
            functools.partial(visibility_kernel, stations, total),
            out_shape=jax.ShapeDtypeStruct((2, owned, 4 * stations * stations), F32),
            in_specs=[VMEM, VMEM],
            out_specs=VMEM,
            name="visibility",
        )(sums, other)
    joined = [jnp.concatenate([blocks[d] for blocks in chunks]) for d in range(stations)]
    joined = jnp.stack(joined)[jnp.arange(stations) ^ lax.axis_index("stn")]
    span = length // stations // cores
    joined = joined.reshape(stations, spectra_here // 4, 2, 2, 2, cores, span, 2, FA)
    joined = jnp.transpose(joined, (4, 2, 1, 7, 3, 0, 5, 6, 8))
    joined = joined.reshape(2, 2, spectra_here, stations * cores, span * FA)
    moved = lax.all_to_all(joined, ("stn", "chan"), split_axis=3, concat_axis=3, tiled=True)
    moved = moved.reshape(2, 2, spectra_here, stations, cores, span * FA)
    moved = jnp.transpose(moved, (0, 3, 1, 4, 2, 5))
    moved = moved.reshape(2, 2 * stations, total, span * FA)
    products = jnp.einsum("xisc,yjsc->xycij", moved, moved, preferred_element_type=F32)
    real_sum = products[0, 0] + products[1, 1]
    imag_sum = products[1, 0] - products[0, 1]
    averaged = jnp.stack([real_sum, imag_sum]) / total
    return averaged.reshape(2, span * FA, 4 * stations * stations)


def solution(mesh):
    in_specs = (P(None, ("grp", "stn"), "chan"), P(None, ("grp", "stn"), None), P())
    out_specs = P(None, ("grp", "stn", "chan"), None)

    return jax.shard_map(shards, mesh=mesh, in_specs=in_specs, out_specs=out_specs, check_vma=False)
```

```python
import functools

import jax
import jax.numpy as jnp
import numpy as np
from jax import lax
from jax.experimental import pallas as pl
from jax.experimental.pallas import tpu as pltpu
from jax.sharding import PartitionSpec as P


FA = 64
LANES = 128
STEP = 8
SHARES = (3, 4, 7, 2)
F32 = jnp.float32
BF16 = jnp.bfloat16
ANY = pl.BlockSpec(memory_space=pl.ANY)
VMEM = pl.BlockSpec(memory_space=pltpu.VMEM)


def cos_sin(index, length):
    angle = (index % length).astype(np.float32) * np.float32(2.0 * np.pi / length)
    return np.cos(angle), np.sin(angle)


def small_tables(length):
    cos, sin = cos_sin(np.outer(np.arange(length), np.arange(length)), length)
    return cos.astype(BF16).astype(np.float32), sin.astype(BF16).astype(np.float32)


def rotation(cos, sin):
    return np.stack([np.stack([cos, sin]), np.stack([-sin, cos])])


def first_table():
    turn = rotation(*small_tables(FA))
    turn = turn.reshape(2, 2, FA // 2, 2, FA)
    table = np.einsum("dchlk,ef->edklchf", turn, np.eye(2))
    return table.reshape(4 * FA, 4 * FA).astype(BF16)


def second_table(length, stations):
    turn = rotation(*small_tables(length)) * (FA * length) ** -0.5
    turn = turn.reshape(2, 2, length, stations, length // stations)
    table = np.einsum("dcbnm,st->nsdmctb", turn, np.eye(2))
    return table.reshape(4 * length, 4 * length).astype(BF16)


def twist_tables(length):
    cos, sin = cos_sin(np.outer(np.arange(FA), np.arange(length)), FA * length)
    return np.stack([np.tile(cos, (1, 2)), np.tile(sin, (1, 2))]).astype(np.float32)


def rows_dot(left, right, axis):
    return lax.dot_general(left, right, (((1,), (axis,)), ((), ())), preferred_element_type=F32)


def spectra_kernel(first, count, taps, stations, last, *refs):
    samples, earlier, passed, prototype, first_hbm, twist_hbm, second_hbm = refs[:7]
    outs = refs[7 : 7 + stations]
    refs = refs[7 + stations :]
    tail = None
    if last:
        tail, refs = refs[0], refs[1:]
    frames, wide, filtered, proto, weights, first_ref, twist_ref, second_in, second, sems = refs
    per = FA
    held = (taps - 1) * per
    total = held + count * per
    tables = [
        pltpu.make_async_copy(source, target, sems.at[at])
        for at, (source, target) in enumerate(
            ((first_hbm, first_ref), (twist_hbm, twist_ref), (second_hbm, second_in))
        )
    ]
    proto_copy = pltpu.make_async_copy(prototype, proto, sems.at[3])
    proto_copy.start()
    lead = 0 if first >= taps - 1 else held
    copies = [
        pltpu.make_async_copy(
            samples.at[comp, pl.ds(first * per - held + lead, total - lead)],
            frames.at[comp, pl.ds(lead, total - lead)],
            sems.at[4 + comp],
        )
        for comp in range(2)
    ]
    for copy in copies + tables:
        copy.start()
    if lead:
        chan = lax.axis_index("chan")
        history = frames.at[:, pl.ds(0, held)]

        @pl.when(chan == 0)
        def _():
            pltpu.make_async_copy(earlier, history, sems.at[6]).start()

        @pl.when(chan != 0)
        def _():
            pltpu.make_async_copy(passed, history, sems.at[6]).start()

        copies.append(pltpu.make_async_copy(earlier, history, sems.at[6]))
    proto_copy.wait()
    for high in range(per // 2):
        for group in range(taps // 8):
            lane = high * LANES
            rows = proto[group * 8 : (group + 1) * 8, lane : lane + LANES]
            for member in range(2):
                at = group * 8 * per + 2 * high + member
                weights[pl.ds(at, 8, stride=per)] = rows
    for copy in copies:
        copy.wait()
    if last:
        tail_copy = pltpu.make_async_copy(
            frames.at[:, pl.ds(count * per, held)], tail, sems.at[6]
        )
        tail_copy.start()

    def widen(frame, carry):
        at = pl.multiple_of(frame * per, per)
        for comp in range(2):
            wide[comp, pl.ds(at, per)] = frames[comp, pl.ds(at, per)].astype(F32)
        return carry

    lax.fori_loop(0, total // per, widen, 0)

    def strip(index, carry):
        comp = index // (per // 16)
        row = (index % (per // 16)) * 16

        def run(block, carry):
            window = []
            for step in range(taps - 1 + STEP):
                at = pl.multiple_of((block * STEP + step) * per + row, 16)
                window.append(wide[comp, pl.ds(at, 16)])
            sums = None
            for tap in range(taps):
                weight = weights[pl.ds(pl.multiple_of(tap * per + row, 16), 16)]
                terms = [weight * window[tap + step] for step in range(STEP)]
                sums = terms if sums is None else [x + y for x, y in zip(sums, terms)]
            for step in range(STEP):
                at = pl.multiple_of(comp * per + row, 16)
                filtered[block * STEP + step, pl.ds(at, 16)] = sums[step].astype(BF16)
            return carry

        return lax.fori_loop(0, count // STEP, run, carry)

    lax.fori_loop(0, 2 * per // 16, strip, 0)
    for copy in tables:
        copy.wait()
    share = second_in.shape[0] // stations
    me = lax.axis_index("stn")
    for offset in range(stations):
        start = pl.multiple_of((me ^ offset) * share, share)
        second[offset * share : (offset + 1) * share] = second_in[pl.ds(start, share)]
    low_half = lax.broadcasted_iota(jnp.int32, (2 * per, LANES), 1) < LANES // 2

    def transform(index, carry):
        mixed = []
        for pair in range(2):
            even = filtered[index * 4 + 2 * pair].astype(F32)
            odd = filtered[index * 4 + 2 * pair + 1].astype(F32)
            low = jnp.where(low_half, even, pltpu.roll(odd, LANES // 2, 1))
            high = jnp.where(low_half, pltpu.roll(even, LANES // 2, 1), odd)
            mixed.append(jnp.concatenate([low.astype(BF16), high.astype(BF16)], axis=0))
        g = rows_dot(first_ref[...], jnp.concatenate(mixed, axis=1), 0)
        cos, sin = twist_ref[0], twist_ref[1]
        inner = []
        for member in range(2):
            for pair in range(2):
                lane = pair * LANES
                g_re = g[2 * member * FA : (2 * member + 1) * FA, lane : lane + LANES]
                g_im = g[(2 * member + 1) * FA : (2 * member + 2) * FA, lane : lane + LANES]
                inner_re = (g_re * cos + g_im * sin).astype(BF16)
                inner_im = (g_im * cos - g_re * sin).astype(BF16)
                inner.append(jnp.concatenate([inner_re, inner_im], axis=1))
        spectra = rows_dot(second[...], jnp.concatenate(inner, axis=0), 1).astype(BF16)
        for member in range(2):
            lane = member * LANES
            for offset in range(stations):
                row = offset * share
                outs[offset][index, member] = spectra[row : row + share, lane : lane + LANES]
        return carry

    lax.fori_loop(0, count // 4, transform, 0, unroll=2 if count % 16 else 4)
    if last:
        tail_copy.wait()


def spectra_of(first, count, samples, earlier, passed, prototype, stations, last):
    taps, channels = prototype.shape
    length = channels // FA
    share = 4 * length // stations
    held = (taps - 1) * FA
    rows = held + count * FA
    tables = (first_table(), twist_tables(length), second_table(length, stations))
    out_shape = [jax.ShapeDtypeStruct((count // 4, 2, share, LANES), BF16)] * stations
    if last:
        out_shape.append(jax.ShapeDtypeStruct((2, held, LANES), BF16))
    return pl.pallas_call(
        functools.partial(spectra_kernel, first, count, taps, stations, last),
        out_shape=out_shape,
        in_specs=[ANY] * 7,
        out_specs=[VMEM] * stations + [ANY] * last,
        scratch_shapes=[
            pltpu.VMEM((2, rows, LANES), BF16),
            pltpu.VMEM((2, rows, LANES), F32),
            pltpu.VMEM((count, 2 * FA, LANES), BF16),
            pltpu.VMEM((taps, channels), F32),
            pltpu.VMEM((taps * FA, LANES), F32),
            pltpu.VMEM((4 * FA, 4 * FA), BF16),
            pltpu.VMEM((2, FA, LANES), F32),
            pltpu.VMEM((4 * length, 4 * length), BF16),
            pltpu.VMEM((4 * length, 4 * length), BF16),
            pltpu.SemaphoreType.DMA((7,)),
        ],
        cost_estimate=pl.CostEstimate(
            flops=count * 8 * 10**6, bytes_accessed=count * 65536, transcendentals=0
        ),
        compiler_params=pltpu.CompilerParams(vmem_limit_bytes=(58 if last else 20) * 2**20),
    )(samples, earlier, passed, prototype, *tables)


def pair_rows(inputs):
    pairs = [(a, b) for a in range(inputs) for b in range(a, inputs)]
    return {pair: row for row, pair in enumerate(pairs)}


def products_kernel(stations, carried, fold, *refs):
    blocks = refs[:stations]
    before = refs[stations] if carried else None
    out = refs[-1]
    rows = pair_rows(2 * stations)
    span = blocks[0].shape[2] // 4
    group = 4

    def load(member, step, low):
        tile = blocks[member // 2][step, member % 2, low * 2 * span : (low + 1) * 2 * span]
        both = tile.astype(F32)
        return both[:span], both[span:]

    for left in range(0, 2 * stations, group):
        for right in range(left, 2 * stations, group):
            a_list = range(left, left + group)
            b_list = range(right, right + group)
            members = [(a, b) for a in a_list for b in b_list if a <= b]
            wanted = [(a, b, comp) for a, b in members for comp in range(2) if a != b or comp == 0]

            def body(step, sums):
                for low in range(2):
                    a_side = {a: load(a, step, low) for a in a_list}
                    b_side = a_side
                    if right != left:
                        b_side = {b: load(b, step, low) for b in b_list}
                    new = []
                    for total, (a, b, comp) in zip(sums, wanted):
                        a_re, a_im = a_side[a]
                        b_re, b_im = b_side[b]
                        if comp == 0:
                            new.append(total + a_re * b_re + a_im * b_im)
                        else:
                            new.append(total + a_im * b_re - a_re * b_im)
                    sums = new
                return sums

            start = []
            for a, b, comp in wanted:
                at = (2 * rows[a, b] + comp) * span
                if carried:
                    start.append(before[at : at + span])
                else:
                    start.append(jnp.zeros((span, LANES), F32))
            sums = lax.fori_loop(0, blocks[0].shape[0], body, start)
            sums = dict(zip(wanted, sums))
            for a, b in members:
                re = sums[a, b, 0]
                im = sums.get((a, b, 1), jnp.zeros_like(re))
                at = rows[a, b] * span
                if fold:
                    low_half = lax.broadcasted_iota(jnp.int32, re.shape, 1) < LANES // 2
                    re = re + pltpu.roll(re, LANES // 2, 1)
                    im = im + pltpu.roll(im, LANES // 2, 1)
                    out[at : at + span] = jnp.where(low_half, re, im)
                else:
                    out[2 * at : 2 * at + span] = re
                    out[2 * at + span : 2 * at + 2 * span] = im


def products_of(blocks, before, fold):
    stations = len(blocks)
    count = len(pair_rows(2 * stations)) * (1 if fold else 2)
    span = blocks[0].shape[2] // 4
    carried = before is not None
    arrays = list(blocks) + ([before] if carried else [])
    steps = 4 * blocks[0].shape[0]
    return pl.pallas_call(
        functools.partial(products_kernel, stations, carried, fold),
        out_shape=jax.ShapeDtypeStruct((count * span, LANES), F32),
        in_specs=[VMEM] * len(arrays),
        out_specs=VMEM,
        cost_estimate=pl.CostEstimate(
            flops=steps * 4 * 10**6, bytes_accessed=steps * 65536, transcendentals=0
        ),
        compiler_params=pltpu.CompilerParams(vmem_limit_bytes=12 * 2**20),
        name="products",
    )(*arrays)


def visibility_kernel(stations, total, own, other, out):
    inputs = 2 * stations
    rows = pair_rows(inputs)
    count = len(rows)
    span = own.shape[0] // count
    mine = span // 2
    width = inputs * inputs
    turn = 2 * lax.axis_index("stn")
    row = lax.broadcasted_iota(jnp.int32, (count, width), 0)
    col = lax.broadcasted_iota(jnp.int32, (count, width), 1)
    i_rel = jnp.zeros_like(row)
    for a in range(1, inputs):
        i_rel = i_rel + (row >= rows[a, a]).astype(jnp.int32)
    j_rel = row - (i_rel * inputs - i_rel * (i_rel - 1) // 2) + i_rel
    i_at, j_at = i_rel ^ turn, j_rel ^ turn
    plain = col == i_at * inputs + j_at
    mirror = col == j_at * inputs + i_at
    picks = [
        jnp.where(plain, 1.0, jnp.where(mirror, sign, 0.0)).astype(BF16) for sign in (1.0, -1.0)
    ]
    core = lax.axis_index("chan")
    for low in range(mine):
        at = pl.ds(core * mine + low, count, stride=span)
        lanes = ((own[at] + other[at]) * (1.0 / total)).T
        for comp in range(2):
            rest = lanes[comp * FA : (comp + 1) * FA]
            value = None
            for _ in range(3):
                piece = rest.astype(BF16)
                part = rows_dot(piece, picks[comp], 0)
                value = part if value is None else value + part
                rest = rest - piece.astype(F32)
            out[comp, low * FA : (low + 1) * FA] = value


def send_order(stations):
    return sorted(range(1, stations), key=lambda d: (d < stations // 2, d))


def shards(voltage, earlier_samples, prototype):
    components, local_inputs, samples = voltage.shape
    _, channels = prototype.shape
    spectra_here = samples // channels
    length = channels // FA
    stations = lax.axis_size("stn")
    cores = lax.axis_size("chan")
    total = spectra_here * cores

    def by_tile(block):
        tiles = block.reshape(components, local_inputs, -1, LANES)
        return jnp.transpose(tiles, (0, 2, 1, 3)).reshape(components, -1, LANES)

    stream = by_tile(voltage)
    earlier = by_tile(earlier_samples)
    whole = sum(SHARES)
    first = spectra_here
    chunks = []
    passed = earlier
    for chunk, share in enumerate(SHARES):
        count = spectra_here * share // whole
        first -= count
        history = earlier if first else passed
        blocks = list(
            spectra_of(
                first, count, stream, earlier, history, prototype, stations, chunk == 0
            )
        )
        if chunk == 0:
            route = [(i, i + 1) for i in range(cores - 1)]
            passed = lax.ppermute(blocks.pop(), "chan", route)
        chunks.append(blocks)
    if 2 * length // stations == 16:
        sums = None
        for chunk, blocks in enumerate(chunks):
            for offset in send_order(stations):
                route = [(i, i ^ offset) for i in range(stations)]
                blocks[offset] = lax.ppermute(blocks[offset], "stn", route)
            sums = products_of(blocks, sums, chunk == len(chunks) - 1)
        other = lax.ppermute(sums, "chan", [(i, i ^ 1) for i in range(cores)])
        owned = channels // (stations * cores)
        return pl.pallas_call(
            functools.partial(visibility_kernel, stations, total),
            out_shape=jax.ShapeDtypeStruct((2, owned, 4 * stations * stations), F32),
            in_specs=[VMEM, VMEM],
            out_specs=VMEM,
            compiler_params=pltpu.CompilerParams(vmem_limit_bytes=12 * 2**20),
            name="visibility",
        )(sums, other)
    joined = [jnp.concatenate([blocks[d] for blocks in chunks]) for d in range(stations)]
    joined = jnp.stack(joined)[jnp.arange(stations) ^ lax.axis_index("stn")]
    span = length // stations // cores
    joined = joined.reshape(stations, spectra_here // 4, 2, 2, 2, cores, span, 2, FA)
    joined = jnp.transpose(joined, (4, 2, 1, 7, 3, 0, 5, 6, 8))
    joined = joined.reshape(2, 2, spectra_here, stations * cores, span * FA)
    moved = lax.all_to_all(joined, ("stn", "chan"), split_axis=3, concat_axis=3, tiled=True)
    moved = moved.reshape(2, 2, spectra_here, stations, cores, span * FA)
    moved = jnp.transpose(moved, (0, 3, 1, 4, 2, 5))
    moved = moved.reshape(2, 2 * stations, total, span * FA)
    products = jnp.einsum("xisc,yjsc->xycij", moved, moved, preferred_element_type=F32)
    real_sum = products[0, 0] + products[1, 1]
    imag_sum = products[1, 0] - products[0, 1]
    averaged = jnp.stack([real_sum, imag_sum]) / total
    return averaged.reshape(2, span * FA, 4 * stations * stations)


def solution(mesh):
    in_specs = (P(None, ("grp", "stn"), "chan"), P(None, ("grp", "stn"), None), P())
    out_specs = P(None, ("grp", "stn", "chan"), None)

    return jax.shard_map(shards, mesh=mesh, in_specs=in_specs, out_specs=out_specs, check_vma=False)
```

```python
import functools

import jax
import jax.numpy as jnp
import numpy as np
from jax import lax
from jax.experimental import pallas as pl
from jax.experimental.pallas import tpu as pltpu
from jax.sharding import PartitionSpec as P


FA = 64
LANES = 128
SUBLANES = 8
STEP = 8
SHARES = (4, 5, 5, 2)
F32 = jnp.float32
BF16 = jnp.bfloat16
ANY = pl.BlockSpec(memory_space=pl.ANY)
VMEM = pl.BlockSpec(memory_space=pltpu.VMEM)


def cos_sin(index, length):
    angle = (index % length).astype(np.float32) * np.float32(2.0 * np.pi / length)
    return np.cos(angle), np.sin(angle)


def small_tables(length):
    cos, sin = cos_sin(np.outer(np.arange(length), np.arange(length)), length)
    return cos.astype(BF16).astype(np.float32), sin.astype(BF16).astype(np.float32)


def rotation(cos, sin):
    return np.stack([np.stack([cos, sin]), np.stack([-sin, cos])])


def first_table():
    turn = rotation(*small_tables(FA))
    turn = turn.reshape(2, 2, FA // 2, 2, FA)
    table = np.einsum("dchlk,ef->edklchf", turn, np.eye(2))
    return table.reshape(4 * FA, 4 * FA).astype(BF16)


def second_table(length, stations, cores=None):
    turn = rotation(*small_tables(length)) * (FA * length) ** -0.5
    turn = turn.reshape(2, 2, length, stations, cores or 1, -1)
    order = "nsdqmctb" if cores is None else "nqdsmctb"
    table = np.einsum("dcbnqm,st->" + order, turn, np.eye(2))
    return table.reshape(4 * length, 4 * length).astype(BF16)


def twist_tables(length):
    cos, sin = cos_sin(np.outer(np.arange(FA), np.arange(length)), FA * length)
    return np.stack([np.tile(cos, (1, 2)), np.tile(sin, (1, 2))]).astype(np.float32)


def rows_dot(left, right, axis):
    return lax.dot_general(left, right, (((1,), (axis,)), ((), ())), preferred_element_type=F32)


def spectra_kernel(first, count, taps, stations, last, split, *refs):
    samples, earlier, passed, prototype, first_hbm, twist_hbm, second_hbm = refs[:7]
    outs = refs[7 : 7 + stations]
    refs = refs[7 + stations :]
    tail = None
    if last or split:
        tail, refs = refs[0], refs[1:]
    frames, wide, filtered, proto, weights, first_ref, twist_ref, second_in, second, sems = refs
    per = FA
    held = (taps - 1) * per
    total = held + count * per
    tables = [
        pltpu.make_async_copy(source, target, sems.at[at])
        for at, (source, target) in enumerate(
            ((first_hbm, first_ref), (twist_hbm, twist_ref), (second_hbm, second_in))
        )
    ]
    proto_copy = pltpu.make_async_copy(prototype, proto, sems.at[3])
    proto_copy.start()
    lead = 0 if first >= taps - 1 else held
    copies = [
        pltpu.make_async_copy(
            samples.at[comp, pl.ds(first * per - held + lead, total - lead)],
            frames.at[comp, pl.ds(lead, total - lead)],
            sems.at[4 + comp],
        )
        for comp in range(2)
    ]
    for copy in copies + tables:
        copy.start()
    if lead:
        chan = lax.axis_index("chan")
        history = frames.at[:, pl.ds(0, held)]

        @pl.when(chan == 0)
        def _():
            pltpu.make_async_copy(earlier, history, sems.at[6]).start()

        @pl.when(chan != 0)
        def _():
            pltpu.make_async_copy(passed, history, sems.at[6]).start()

        copies.append(pltpu.make_async_copy(earlier, history, sems.at[6]))
    proto_copy.wait()
    for high in range(per // 2):
        for group in range(taps // 8):
            lane = high * LANES
            rows = proto[group * 8 : (group + 1) * 8, lane : lane + LANES]
            for member in range(2):
                at = group * 8 * per + 2 * high + member
                weights[pl.ds(at, 8, stride=per)] = rows
    for copy in copies:
        copy.wait()
    if last:
        tail_copy = pltpu.make_async_copy(
            frames.at[:, pl.ds(count * per, held)], tail, sems.at[6]
        )
        tail_copy.start()

    def widen(frame, carry):
        at = pl.multiple_of(frame * per, per)
        for comp in range(2):
            wide[comp, pl.ds(at, per)] = frames[comp, pl.ds(at, per)].astype(F32)
        return carry

    lax.fori_loop(0, total // per, widen, 0)

    def strip(index, carry):
        comp = index // (per // 16)
        row = (index % (per // 16)) * 16

        def run(block, carry):
            window = []
            for step in range(taps - 1 + STEP):
                at = pl.multiple_of((block * STEP + step) * per + row, 16)
                window.append(wide[comp, pl.ds(at, 16)])
            sums = None
            for tap in range(taps):
                weight = weights[pl.ds(pl.multiple_of(tap * per + row, 16), 16)]
                terms = [weight * window[tap + step] for step in range(STEP)]
                sums = terms if sums is None else [x + y for x, y in zip(sums, terms)]
            for step in range(STEP):
                at = pl.multiple_of(comp * per + row, 16)
                filtered[block * STEP + step, pl.ds(at, 16)] = sums[step].astype(BF16)
            return carry

        return lax.fori_loop(0, count // STEP, run, carry)

    lax.fori_loop(0, 2 * per // 16, strip, 0)
    for copy in tables:
        copy.wait()
    share = second_in.shape[0] // stations
    me = lax.axis_index("stn")
    parts = 2 if split else 1
    block = share // parts
    for part in range(parts):
        core = (lax.axis_index("chan") ^ part) * block if split else 0
        for offset in range(stations):
            start = pl.multiple_of((me ^ offset) * share + core, block)
            at = (part * stations + offset) * block
            second[at : at + block] = second_in[pl.ds(start, block)]
    low_half = lax.broadcasted_iota(jnp.int32, (2 * per, LANES), 1) < LANES // 2

    def transform(index, carry):
        mixed = []
        for pair in range(2):
            even = filtered[index * 4 + 2 * pair].astype(F32)
            odd = filtered[index * 4 + 2 * pair + 1].astype(F32)
            low = jnp.where(low_half, even, pltpu.roll(odd, LANES // 2, 1))
            high = jnp.where(low_half, pltpu.roll(even, LANES // 2, 1), odd)
            mixed.append(jnp.concatenate([low.astype(BF16), high.astype(BF16)], axis=0))
        g = rows_dot(first_ref[...], jnp.concatenate(mixed, axis=1), 0)
        cos, sin = twist_ref[0], twist_ref[1]
        inner = []
        for member in range(2):
            for pair in range(2):
                lane = pair * LANES
                g_re = g[2 * member * FA : (2 * member + 1) * FA, lane : lane + LANES]
                g_im = g[(2 * member + 1) * FA : (2 * member + 2) * FA, lane : lane + LANES]
                inner_re = (g_re * cos + g_im * sin).astype(BF16)
                inner_im = (g_im * cos - g_re * sin).astype(BF16)
                inner.append(jnp.concatenate([inner_re, inner_im], axis=1))
        spectra = rows_dot(second[...], jnp.concatenate(inner, axis=0), 1).astype(BF16)
        for member in range(2):
            lane = member * LANES
            for offset in range(stations):
                row = offset * block
                outs[offset][index, member] = spectra[row : row + block, lane : lane + LANES]
                if split:
                    row = (stations + offset) * block
                    tail[offset, index, member] = spectra[row : row + block, lane : lane + LANES]
        return carry

    lax.fori_loop(0, count // 4, transform, 0, unroll=2 if count % 16 else 4)
    if last:
        tail_copy.wait()


def spectra_of(first, count, samples, earlier, passed, prototype, stations, last, cores=None):
    taps, channels = prototype.shape
    length = channels // FA
    share = 4 * length // stations
    held = (taps - 1) * FA
    rows = held + count * FA
    tables = (first_table(), twist_tables(length), second_table(length, stations, cores))
    sent = (count // 4, 2, share // (cores or 1), LANES)
    out_shape = [jax.ShapeDtypeStruct(sent, BF16)] * stations
    if cores:
        out_shape.append(jax.ShapeDtypeStruct((stations,) + sent, BF16))
    if last:
        out_shape.append(jax.ShapeDtypeStruct((2, held, LANES), BF16))
    return pl.pallas_call(
        functools.partial(spectra_kernel, first, count, taps, stations, last, bool(cores)),
        out_shape=out_shape,
        in_specs=[ANY] * 7,
        out_specs=[VMEM] * stations + [ANY] * last + [VMEM] * bool(cores),
        scratch_shapes=[
            pltpu.VMEM((2, rows, LANES), BF16),
            pltpu.VMEM((2, rows, LANES), F32),
            pltpu.VMEM((count, 2 * FA, LANES), BF16),
            pltpu.VMEM((taps, channels), F32),
            pltpu.VMEM((taps * FA, LANES), F32),
            pltpu.VMEM((4 * FA, 4 * FA), BF16),
            pltpu.VMEM((2, FA, LANES), F32),
            pltpu.VMEM((4 * length, 4 * length), BF16),
            pltpu.VMEM((4 * length, 4 * length), BF16),
            pltpu.SemaphoreType.DMA((7,)),
        ],
        cost_estimate=pl.CostEstimate(
            flops=count * 8 * 10**6, bytes_accessed=count * 65536, transcendentals=0
        ),
        compiler_params=pltpu.CompilerParams(vmem_limit_bytes=(58 if last else 20) * 2**20),
    )(samples, earlier, passed, prototype, *tables)


def join_kernel(stations, *refs):
    mine, twin, outs = refs[:stations], refs[stations], refs[stations + 1 :]
    half = mine[0].shape[0]
    for offset in range(stations):
        outs[offset][:half] = mine[offset][...]
        outs[offset][half:] = twin[offset]


def join(mine, twin):
    shape = (2 * mine[0].shape[0],) + mine[0].shape[1:]
    return pl.pallas_call(
        functools.partial(join_kernel, len(mine)),
        out_shape=[jax.ShapeDtypeStruct(shape, BF16)] * len(mine),
        in_specs=[VMEM] * (len(mine) + 1),
        out_specs=[VMEM] * len(mine),
        compiler_params=pltpu.CompilerParams(vmem_limit_bytes=12 * 2**20),
        cost_estimate=pl.CostEstimate(flops=10**6, bytes_accessed=10**6, transcendentals=0),
        name="join",
    )(*mine, twin)


def pair_rows(inputs):
    pairs = [(a, b) for a in range(inputs) for b in range(a, inputs)]
    return {pair: row for row, pair in enumerate(pairs)}


def products_kernel(stations, carried, fold, *refs):
    blocks = refs[:stations]
    before = refs[stations] if carried else None
    out = refs[-1]
    rows = pair_rows(2 * stations)
    span = SUBLANES
    group = 4

    def load(member, step, low):
        tile = blocks[member // 2][step, member % 2, low * 2 * span : (low + 1) * 2 * span]
        both = tile.astype(F32)
        return both[:span], both[span:]

    for left in range(0, 2 * stations, group):
        for right in range(left, 2 * stations, group):
            a_list = range(left, left + group)
            b_list = range(right, right + group)
            members = [(a, b) for a in a_list for b in b_list if a <= b]
            wanted = [(a, b, comp) for a, b in members for comp in range(2) if a != b or comp == 0]

            def body(step, sums):
                for low in range(blocks[0].shape[2] // (2 * span)):
                    a_side = {a: load(a, step, low) for a in a_list}
                    b_side = a_side
                    if right != left:
                        b_side = {b: load(b, step, low) for b in b_list}
                    new = []
                    for total, (a, b, comp) in zip(sums, wanted):
                        a_re, a_im = a_side[a]
                        b_re, b_im = b_side[b]
                        if comp == 0:
                            new.append(total + a_re * b_re + a_im * b_im)
                        else:
                            new.append(total + a_im * b_re - a_re * b_im)
                    sums = new
                return sums

            start = []
            for a, b, comp in wanted:
                at = (2 * rows[a, b] + comp) * span
                if carried:
                    start.append(before[at : at + span])
                else:
                    start.append(jnp.zeros((span, LANES), F32))
            sums = lax.fori_loop(0, blocks[0].shape[0], body, start)
            sums = dict(zip(wanted, sums))
            for a, b in members:
                re = sums[a, b, 0]
                im = sums.get((a, b, 1), jnp.zeros_like(re))
                at = rows[a, b] * span
                if fold:
                    low_half = lax.broadcasted_iota(jnp.int32, re.shape, 1) < LANES // 2
                    re = re + pltpu.roll(re, LANES // 2, 1)
                    im = im + pltpu.roll(im, LANES // 2, 1)
                    out[at : at + span] = jnp.where(low_half, re, im)
                else:
                    out[2 * at : 2 * at + span] = re
                    out[2 * at + span : 2 * at + 2 * span] = im


def products_of(blocks, before, fold):
    stations = len(blocks)
    count = len(pair_rows(2 * stations)) * (1 if fold else 2)
    span = SUBLANES
    carried = before is not None
    arrays = list(blocks) + ([before] if carried else [])
    steps = blocks[0].shape[0] * blocks[0].shape[2] // 8
    return pl.pallas_call(
        functools.partial(products_kernel, stations, carried, fold),
        out_shape=jax.ShapeDtypeStruct((count * span, LANES), F32),
        in_specs=[VMEM] * len(arrays),
        out_specs=VMEM,
        cost_estimate=pl.CostEstimate(
            flops=steps * 4 * 10**6, bytes_accessed=steps * 65536, transcendentals=0
        ),
        compiler_params=pltpu.CompilerParams(vmem_limit_bytes=12 * 2**20),
        name="products",
    )(*arrays)


def visibility_kernel(stations, total, own, other, late, out):
    inputs = 2 * stations
    rows = pair_rows(inputs)
    count = len(rows)
    span = own.shape[0] // count
    mine = span // 2
    width = inputs * inputs
    turn = 2 * lax.axis_index("stn")
    row = lax.broadcasted_iota(jnp.int32, (count, width), 0)
    col = lax.broadcasted_iota(jnp.int32, (count, width), 1)
    i_rel = jnp.zeros_like(row)
    for a in range(1, inputs):
        i_rel = i_rel + (row >= rows[a, a]).astype(jnp.int32)
    j_rel = row - (i_rel * inputs - i_rel * (i_rel - 1) // 2) + i_rel
    i_at, j_at = i_rel ^ turn, j_rel ^ turn
    plain = col == i_at * inputs + j_at
    mirror = col == j_at * inputs + i_at
    picks = [
        jnp.where(plain, 1.0, jnp.where(mirror, sign, 0.0)).astype(BF16) for sign in (1.0, -1.0)
    ]
    core = lax.axis_index("chan")
    for low in range(mine):
        at = pl.ds(core * mine + low, count, stride=span)
        both = own[at] + other[at]
        for half in range(2):
            both = both + late[pl.ds(half * mine + low, count, stride=span)]
        lanes = (both * (1.0 / total)).T
        for comp in range(2):
            rest = lanes[comp * FA : (comp + 1) * FA]
            value = None
            for _ in range(3):
                piece = rest.astype(BF16)
                part = rows_dot(piece, picks[comp], 0)
                value = part if value is None else value + part
                rest = rest - piece.astype(F32)
            out[comp, low * FA : (low + 1) * FA] = value


def send_order(stations):
    return sorted(range(1, stations), key=lambda d: (d < stations // 2, d))


def shards(voltage, earlier_samples, prototype):
    components, local_inputs, samples = voltage.shape
    _, channels = prototype.shape
    spectra_here = samples // channels
    length = channels // FA
    stations = lax.axis_size("stn")
    cores = lax.axis_size("chan")
    total = spectra_here * cores

    def by_tile(block):
        tiles = block.reshape(components, local_inputs, -1, LANES)
        return jnp.transpose(tiles, (0, 2, 1, 3)).reshape(components, -1, LANES)

    stream = by_tile(voltage)
    earlier = by_tile(earlier_samples)
    whole = sum(SHARES)
    staged = length // stations == SUBLANES
    first = spectra_here
    chunks = []
    passed = earlier
    for chunk, share in enumerate(SHARES):
        count = spectra_here * share // whole
        first -= count
        history = earlier if first else passed
        blocks = list(
            spectra_of(
                first,
                count,
                stream,
                earlier,
                history,
                prototype,
                stations,
                chunk == 0,
                cores if staged and first == 0 else None,
            )
        )
        if chunk == 0:
            route = [(i, i + 1) for i in range(cores - 1)]
            passed = lax.ppermute(blocks.pop(), "chan", route)
        chunks.append(blocks)
    if staged:
        swap = [(i, i ^ 1) for i in range(cores)]
        sums = None
        for chunk, blocks in enumerate(chunks):
            late = chunk == len(chunks) - 1
            if late:
                twin = lax.ppermute(blocks.pop(), "chan", swap)
                blocks = list(join(blocks, twin))
            for offset in send_order(stations):
                route = [(i, i ^ offset) for i in range(stations)]
                blocks[offset] = lax.ppermute(blocks[offset], "stn", route)
            if late:
                newest = products_of(blocks, None, True)
            else:
                sums = products_of(blocks, sums, chunk == len(chunks) - 2)
        other = lax.ppermute(sums, "chan", swap)
        owned = channels // (stations * cores)
        return pl.pallas_call(
            functools.partial(visibility_kernel, stations, total),
            out_shape=jax.ShapeDtypeStruct((2, owned, 4 * stations * stations), F32),
            in_specs=[VMEM] * 3,
            out_specs=VMEM,
            compiler_params=pltpu.CompilerParams(vmem_limit_bytes=12 * 2**20),
            name="visibility",
        )(sums, other, newest)
    joined = [jnp.concatenate([blocks[d] for blocks in chunks]) for d in range(stations)]
    joined = jnp.stack(joined)[jnp.arange(stations) ^ lax.axis_index("stn")]
    span = length // stations // cores
    joined = joined.reshape(stations, spectra_here // 4, 2, 2, 2, cores, span, 2, FA)
    joined = jnp.transpose(joined, (4, 2, 1, 7, 3, 0, 5, 6, 8))
    joined = joined.reshape(2, 2, spectra_here, stations * cores, span * FA)
    moved = lax.all_to_all(joined, ("stn", "chan"), split_axis=3, concat_axis=3, tiled=True)
    moved = moved.reshape(2, 2, spectra_here, stations, cores, span * FA)
    moved = jnp.transpose(moved, (0, 3, 1, 4, 2, 5))
    moved = moved.reshape(2, 2 * stations, total, span * FA)
    products = jnp.einsum("xisc,yjsc->xycij", moved, moved, preferred_element_type=F32)
    real_sum = products[0, 0] + products[1, 1]
    imag_sum = products[1, 0] - products[0, 1]
    averaged = jnp.stack([real_sum, imag_sum]) / total
    return averaged.reshape(2, span * FA, 4 * stations * stations)


def solution(mesh):
    in_specs = (P(None, ("grp", "stn"), "chan"), P(None, ("grp", "stn"), None), P())
    out_specs = P(None, ("grp", "stn", "chan"), None)

    return jax.shard_map(shards, mesh=mesh, in_specs=in_specs, out_specs=out_specs, check_vma=False)
```

```python
import functools

import jax
import jax.numpy as jnp
import numpy as np
from jax import lax
from jax.experimental import pallas as pl
from jax.experimental.pallas import tpu as pltpu
from jax.sharding import PartitionSpec as P


FA = 64
LANES = 128
SUBLANES = 8
STEP = 8
SHARES = (4, 5, 5, 2)
F32 = jnp.float32
BF16 = jnp.bfloat16
ANY = pl.BlockSpec(memory_space=pl.ANY)
VMEM = pl.BlockSpec(memory_space=pltpu.VMEM)


def cos_sin(index, length):
    angle = (index % length).astype(np.float32) * np.float32(2.0 * np.pi / length)
    return np.cos(angle), np.sin(angle)


def small_tables(length):
    cos, sin = cos_sin(np.outer(np.arange(length), np.arange(length)), length)
    return cos.astype(BF16).astype(np.float32), sin.astype(BF16).astype(np.float32)


def rotation(cos, sin):
    return np.stack([np.stack([cos, sin]), np.stack([-sin, cos])])


def first_table():
    turn = rotation(*small_tables(FA))
    turn = turn.reshape(2, 2, FA // 2, 2, FA)
    table = np.einsum("dchlk,ef->edklchf", turn, np.eye(2))
    return table.reshape(4 * FA, 4 * FA).astype(BF16)


def second_table(length, stations, cores=None):
    turn = rotation(*small_tables(length)) * (FA * length) ** -0.5
    turn = turn.reshape(2, 2, length, stations, cores or 1, -1)
    order = "nsdqmctb" if cores is None else "nqdsmctb"
    table = np.einsum("dcbnqm,st->" + order, turn, np.eye(2))
    return table.reshape(4 * length, 4 * length).astype(BF16)


def twist_tables(length):
    cos, sin = cos_sin(np.outer(np.arange(FA), np.arange(length)), FA * length)
    return np.stack([np.tile(cos, (1, 2)), np.tile(sin, (1, 2))]).astype(np.float32)


def rows_dot(left, right, axis):
    return lax.dot_general(left, right, (((1,), (axis,)), ((), ())), preferred_element_type=F32)


def spectra_kernel(first, count, taps, stations, last, split, *refs):
    samples, earlier, passed, prototype, first_hbm, twist_hbm, second_hbm = refs[:7]
    outs = refs[7 : 7 + stations]
    refs = refs[7 + stations :]
    tail = None
    if last or split:
        tail, refs = refs[0], refs[1:]
    frames, wide, filtered, proto, weights, first_ref, twist_ref, second_in, second, sems = refs
    per = FA
    held = (taps - 1) * per
    total = held + count * per
    tables = [
        pltpu.make_async_copy(source, target, sems.at[at])
        for at, (source, target) in enumerate(
            ((first_hbm, first_ref), (twist_hbm, twist_ref), (second_hbm, second_in))
        )
    ]
    proto_copy = pltpu.make_async_copy(prototype, proto, sems.at[3])
    proto_copy.start()
    lead = 0 if first >= taps - 1 else held
    copies = [
        pltpu.make_async_copy(
            samples.at[comp, pl.ds(first * per - held + lead, total - lead)],
            frames.at[comp, pl.ds(lead, total - lead)],
            sems.at[4 + comp],
        )
        for comp in range(2)
    ]
    for copy in copies + tables:
        copy.start()
    if lead:
        chan = lax.axis_index("chan")
        history = frames.at[:, pl.ds(0, held)]

        @pl.when(chan == 0)
        def _():
            pltpu.make_async_copy(earlier, history, sems.at[6]).start()

        @pl.when(chan != 0)
        def _():
            pltpu.make_async_copy(passed, history, sems.at[6]).start()

        copies.append(pltpu.make_async_copy(earlier, history, sems.at[6]))
    proto_copy.wait()
    for high in range(per // 2):
        for group in range(taps // 8):
            lane = high * LANES
            rows = proto[group * 8 : (group + 1) * 8, lane : lane + LANES]
            for member in range(2):
                at = group * 8 * per + 2 * high + member
                weights[pl.ds(at, 8, stride=per)] = rows
    for copy in copies:
        copy.wait()
    if last:
        tail_copy = pltpu.make_async_copy(
            frames.at[:, pl.ds(count * per, held)], tail, sems.at[6]
        )
        tail_copy.start()

    def widen(frame, carry):
        at = pl.multiple_of(frame * per, per)
        for comp in range(2):
            wide[comp, pl.ds(at, per)] = frames[comp, pl.ds(at, per)].astype(F32)
        return carry

    lax.fori_loop(0, total // per, widen, 0)

    def strip(index, carry):
        comp = index // (per // 16)
        row = (index % (per // 16)) * 16

        def run(block, carry):
            window = []
            for step in range(taps - 1 + STEP):
                at = pl.multiple_of((block * STEP + step) * per + row, 16)
                window.append(wide[comp, pl.ds(at, 16)])
            sums = None
            for tap in range(taps):
                weight = weights[pl.ds(pl.multiple_of(tap * per + row, 16), 16)]
                terms = [weight * window[tap + step] for step in range(STEP)]
                sums = terms if sums is None else [x + y for x, y in zip(sums, terms)]
            for step in range(STEP):
                at = pl.multiple_of(comp * per + row, 16)
                filtered[block * STEP + step, pl.ds(at, 16)] = sums[step].astype(BF16)
            return carry

        return lax.fori_loop(0, count // STEP, run, carry)

    lax.fori_loop(0, 2 * per // 16, strip, 0)
    for copy in tables:
        copy.wait()
    share = second_in.shape[0] // stations
    me = lax.axis_index("stn")
    parts = 2 if split else 1
    block = share // parts
    for part in range(parts):
        core = (lax.axis_index("chan") ^ part) * block if split else 0
        for offset in range(stations):
            start = pl.multiple_of((me ^ offset) * share + core, block)
            at = (part * stations + offset) * block
            second[at : at + block] = second_in[pl.ds(start, block)]
    low_half = lax.broadcasted_iota(jnp.int32, (2 * per, LANES), 1) < LANES // 2

    def transform(index, carry):
        mixed = []
        for pair in range(2):
            even = filtered[index * 4 + 2 * pair].astype(F32)
            odd = filtered[index * 4 + 2 * pair + 1].astype(F32)
            low = jnp.where(low_half, even, pltpu.roll(odd, LANES // 2, 1))
            high = jnp.where(low_half, pltpu.roll(even, LANES // 2, 1), odd)
            mixed.append(jnp.concatenate([low.astype(BF16), high.astype(BF16)], axis=0))
        g = rows_dot(first_ref[...], jnp.concatenate(mixed, axis=1), 0)
        cos, sin = twist_ref[0], twist_ref[1]
        inner = []
        for member in range(2):
            for pair in range(2):
                lane = pair * LANES
                g_re = g[2 * member * FA : (2 * member + 1) * FA, lane : lane + LANES]
                g_im = g[(2 * member + 1) * FA : (2 * member + 2) * FA, lane : lane + LANES]
                inner_re = (g_re * cos + g_im * sin).astype(BF16)
                inner_im = (g_im * cos - g_re * sin).astype(BF16)
                inner.append(jnp.concatenate([inner_re, inner_im], axis=1))
        spectra = rows_dot(second[...], jnp.concatenate(inner, axis=0), 1).astype(BF16)
        for member in range(2):
            lane = member * LANES
            for offset in range(stations):
                row = offset * block
                outs[offset][index, member] = spectra[row : row + block, lane : lane + LANES]
                if split:
                    row = (stations + offset) * block
                    tail[offset, index, member] = spectra[row : row + block, lane : lane + LANES]
        return carry

    lax.fori_loop(0, count // 4, transform, 0, unroll=2 if count % 16 else 4)
    if last:
        tail_copy.wait()


def spectra_of(first, count, samples, earlier, passed, prototype, stations, last, cores=None):
    taps, channels = prototype.shape
    length = channels // FA
    share = 4 * length // stations
    held = (taps - 1) * FA
    rows = held + count * FA
    tables = (first_table(), twist_tables(length), second_table(length, stations, cores))
    sent = (count // 4, 2, share // (cores or 1), LANES)
    out_shape = [jax.ShapeDtypeStruct(sent, BF16)] * stations
    if cores:
        out_shape.append(jax.ShapeDtypeStruct((stations,) + sent, BF16))
    if last:
        out_shape.append(jax.ShapeDtypeStruct((2, held, LANES), BF16))
    return pl.pallas_call(
        functools.partial(spectra_kernel, first, count, taps, stations, last, bool(cores)),
        out_shape=out_shape,
        in_specs=[ANY] * 7,
        out_specs=[VMEM] * stations + [ANY] * last + [VMEM] * bool(cores),
        scratch_shapes=[
            pltpu.VMEM((2, rows, LANES), BF16),
            pltpu.VMEM((2, rows, LANES), F32),
            pltpu.VMEM((count, 2 * FA, LANES), BF16),
            pltpu.VMEM((taps, channels), F32),
            pltpu.VMEM((taps * FA, LANES), F32),
            pltpu.VMEM((4 * FA, 4 * FA), BF16),
            pltpu.VMEM((2, FA, LANES), F32),
            pltpu.VMEM((4 * length, 4 * length), BF16),
            pltpu.VMEM((4 * length, 4 * length), BF16),
            pltpu.SemaphoreType.DMA((7,)),
        ],
        cost_estimate=pl.CostEstimate(
            flops=count * 8 * 10**6, bytes_accessed=count * 65536, transcendentals=0
        ),
        compiler_params=pltpu.CompilerParams(vmem_limit_bytes=(58 if last else 20) * 2**20),
    )(samples, earlier, passed, prototype, *tables)


def join_kernel(stations, *refs):
    mine, twin, outs = refs[:stations], refs[stations], refs[stations + 1 :]
    half = mine[0].shape[0]
    for offset in range(stations):
        outs[offset][:half] = mine[offset][...]
        outs[offset][half:] = twin[offset]


def join(mine, twin):
    shape = (2 * mine[0].shape[0],) + mine[0].shape[1:]
    return pl.pallas_call(
        functools.partial(join_kernel, len(mine)),
        out_shape=[jax.ShapeDtypeStruct(shape, BF16)] * len(mine),
        in_specs=[VMEM] * (len(mine) + 1),
        out_specs=[VMEM] * len(mine),
        compiler_params=pltpu.CompilerParams(vmem_limit_bytes=12 * 2**20),
        cost_estimate=pl.CostEstimate(flops=10**6, bytes_accessed=10**6, transcendentals=0),
        name="join",
    )(*mine, twin)


def pair_rows(inputs):
    pairs = [(a, b) for a in range(inputs) for b in range(a, inputs)]
    return {pair: row for row, pair in enumerate(pairs)}


def products_kernel(inputs, carried, part, *refs):
    before = refs[-2] if carried else None
    blocks = refs[: -2 if carried else -1]
    out = refs[-1]
    rows = pair_rows(inputs)
    span = SUBLANES
    group = 4
    last = inputs - group

    def load(member, step, low):
        tile = blocks[member // 2][step, member % 2, low * 2 * span : (low + 1) * 2 * span]
        both = tile.astype(F32)
        return both[:span], both[span:]

    for left in range(0, inputs, group):
        for right in range(left, inputs, group):
            a_list = range(left, left + group)
            b_list = range(right, right + group)
            members = [(a, b) for a in a_list for b in b_list if a <= b]
            wanted = [(a, b, comp) for a, b in members for comp in range(2) if a != b or comp == 0]
            active = part == "all" or (part == "early") == (right < last)
            known = carried and (part != "late" or right < last or carried == 2)
            if not (active or known):
                continue

            def body(step, sums):
                for low in range(blocks[0].shape[2] // (2 * span)):
                    a_side = {a: load(a, step, low) for a in a_list}
                    b_side = a_side
                    if right != left:
                        b_side = {b: load(b, step, low) for b in b_list}
                    new = []
                    for total, (a, b, comp) in zip(sums, wanted):
                        a_re, a_im = a_side[a]
                        b_re, b_im = b_side[b]
                        if comp == 0:
                            new.append(total + a_re * b_re + a_im * b_im)
                        else:
                            new.append(total + a_im * b_re - a_re * b_im)
                    sums = new
                return sums

            sums = []
            for a, b, comp in wanted:
                at = (2 * rows[a, b] + comp) * span
                sums.append(before[at : at + span] if known else jnp.zeros((span, LANES), F32))
            if active:
                sums = lax.fori_loop(0, blocks[0].shape[0], body, sums)
            sums = dict(zip(wanted, sums))
            for a, b in members:
                re = sums[a, b, 0]
                im = sums.get((a, b, 1), jnp.zeros_like(re))
                at = rows[a, b] * span
                if part == "late":
                    low_half = lax.broadcasted_iota(jnp.int32, re.shape, 1) < LANES // 2
                    re = re + pltpu.roll(re, LANES // 2, 1)
                    im = im + pltpu.roll(im, LANES // 2, 1)
                    out[at : at + span] = jnp.where(low_half, re, im)
                else:
                    out[2 * at : 2 * at + span] = re
                    out[2 * at + span : 2 * at + 2 * span] = im


def products_of(blocks, before, part="all", whole=True):
    inputs = 2 * len(blocks)
    count = len(pair_rows(inputs)) * (1 if part == "late" else 2)
    carried = 0 if before is None else 1 + whole
    used = blocks[:-2] if part == "early" else blocks
    arrays = list(used) + ([before] if carried else [])
    steps = blocks[0].shape[0] * blocks[0].shape[2] // 8
    return pl.pallas_call(
        functools.partial(products_kernel, inputs, carried, part),
        out_shape=jax.ShapeDtypeStruct((count * SUBLANES, LANES), F32),
        in_specs=[VMEM] * len(arrays),
        out_specs=VMEM,
        compiler_params=pltpu.CompilerParams(vmem_limit_bytes=12 * 2**20),
        cost_estimate=pl.CostEstimate(
            flops=steps * 4 * 10**6, bytes_accessed=steps * 65536, transcendentals=0
        ),
    )(*arrays)


def visibility_kernel(stations, total, own, other, late, out):
    inputs = 2 * stations
    rows = pair_rows(inputs)
    count = len(rows)
    span = own.shape[0] // count
    mine = span // 2
    width = inputs * inputs
    turn = 2 * lax.axis_index("stn")
    row = lax.broadcasted_iota(jnp.int32, (count, width), 0)
    col = lax.broadcasted_iota(jnp.int32, (count, width), 1)
    i_rel = jnp.zeros_like(row)
    for a in range(1, inputs):
        i_rel = i_rel + (row >= rows[a, a]).astype(jnp.int32)
    j_rel = row - (i_rel * inputs - i_rel * (i_rel - 1) // 2) + i_rel
    i_at, j_at = i_rel ^ turn, j_rel ^ turn
    plain = col == i_at * inputs + j_at
    mirror = col == j_at * inputs + i_at
    picks = [
        jnp.where(plain, 1.0, jnp.where(mirror, sign, 0.0)).astype(BF16) for sign in (1.0, -1.0)
    ]
    core = lax.axis_index("chan")
    for low in range(mine):
        at = pl.ds(core * mine + low, count, stride=span)
        both = own[at] + other[at]
        for half in range(2):
            both = both + late[pl.ds(half * mine + low, count, stride=span)]
        lanes = (both * (1.0 / total)).T
        for comp in range(2):
            rest = lanes[comp * FA : (comp + 1) * FA]
            value = None
            for _ in range(3):
                piece = rest.astype(BF16)
                part = rows_dot(piece, picks[comp], 0)
                value = part if value is None else value + part
                rest = rest - piece.astype(F32)
            out[comp, low * FA : (low + 1) * FA] = value


def send_order(stations):
    return sorted(range(1, stations), key=lambda d: (d < stations // 2, d))


def shards(voltage, earlier_samples, prototype):
    components, local_inputs, samples = voltage.shape
    _, channels = prototype.shape
    spectra_here = samples // channels
    length = channels // FA
    stations = lax.axis_size("stn")
    cores = lax.axis_size("chan")
    total = spectra_here * cores

    def by_tile(block):
        tiles = block.reshape(components, local_inputs, -1, LANES)
        return jnp.transpose(tiles, (0, 2, 1, 3)).reshape(components, -1, LANES)

    stream = by_tile(voltage)
    earlier = by_tile(earlier_samples)
    whole = sum(SHARES)
    staged = length // stations == SUBLANES
    first = spectra_here
    chunks = []
    passed = earlier
    for chunk, share in enumerate(SHARES):
        count = spectra_here * share // whole
        first -= count
        history = earlier if first else passed
        blocks = list(
            spectra_of(
                first,
                count,
                stream,
                earlier,
                history,
                prototype,
                stations,
                chunk == 0,
                cores if staged and first == 0 else None,
            )
        )
        if chunk == 0:
            route = [(i, i + 1) for i in range(cores - 1)]
            passed = lax.ppermute(blocks.pop(), "chan", route)
        chunks.append(blocks)
    if staged:
        swap = [(i, i ^ 1) for i in range(cores)]
        sums = None
        for chunk, blocks in enumerate(chunks):
            late = chunk == len(chunks) - 1
            if late:
                twin = lax.ppermute(blocks.pop(), "chan", swap)
                blocks = list(join(blocks, twin))
            for offset in send_order(stations):
                route = [(i, i ^ offset) for i in range(stations)]
                blocks[offset] = lax.ppermute(blocks[offset], "stn", route)
            if chunk < len(chunks) - 2:
                sums = products_of(blocks, sums)
                continue
            start = None if late else sums
            early = products_of(blocks, start, "early")
            newest = products_of(blocks, early, "late", not late)
            if not late:
                sums = newest
        other = lax.ppermute(sums, "chan", swap)
        owned = channels // (stations * cores)
        return pl.pallas_call(
            functools.partial(visibility_kernel, stations, total),
            out_shape=jax.ShapeDtypeStruct((2, owned, 4 * stations * stations), F32),
            in_specs=[VMEM] * 3,
            out_specs=VMEM,
            compiler_params=pltpu.CompilerParams(vmem_limit_bytes=12 * 2**20),
            name="visibility",
        )(sums, other, newest)
    joined = [jnp.concatenate([blocks[d] for blocks in chunks]) for d in range(stations)]
    joined = jnp.stack(joined)[jnp.arange(stations) ^ lax.axis_index("stn")]
    span = length // stations // cores
    joined = joined.reshape(stations, spectra_here // 4, 2, 2, 2, cores, span, 2, FA)
    joined = jnp.transpose(joined, (4, 2, 1, 7, 3, 0, 5, 6, 8))
    joined = joined.reshape(2, 2, spectra_here, stations * cores, span * FA)
    moved = lax.all_to_all(joined, ("stn", "chan"), split_axis=3, concat_axis=3, tiled=True)
    moved = moved.reshape(2, 2, spectra_here, stations, cores, span * FA)
    moved = jnp.transpose(moved, (0, 3, 1, 4, 2, 5))
    moved = moved.reshape(2, 2 * stations, total, span * FA)
    products = jnp.einsum("xisc,yjsc->xycij", moved, moved, preferred_element_type=F32)
    real_sum = products[0, 0] + products[1, 1]
    imag_sum = products[1, 0] - products[0, 1]
    averaged = jnp.stack([real_sum, imag_sum]) / total
    return averaged.reshape(2, span * FA, 4 * stations * stations)


def solution(mesh):
    in_specs = (P(None, ("grp", "stn"), "chan"), P(None, ("grp", "stn"), None), P())
    out_specs = P(None, ("grp", "stn", "chan"), None)

    return jax.shard_map(shards, mesh=mesh, in_specs=in_specs, out_specs=out_specs, check_vma=False)
```

```python
import functools

import jax
import jax.numpy as jnp
import numpy as np
from jax import lax
from jax.experimental import pallas as pl
from jax.experimental.pallas import tpu as pltpu
from jax.sharding import PartitionSpec as P


FA = 64
LANES = 128
SUBLANES = 8
STEP = 8
SHARES = (4, 5, 5, 2)
F32 = jnp.float32
BF16 = jnp.bfloat16
ANY = pl.BlockSpec(memory_space=pl.ANY)
VMEM = pl.BlockSpec(memory_space=pltpu.VMEM)


def cos_sin(index, length):
    angle = (index % length).astype(np.float32) * np.float32(2.0 * np.pi / length)
    return np.cos(angle), np.sin(angle)


def small_tables(length):
    cos, sin = cos_sin(np.outer(np.arange(length), np.arange(length)), length)
    return cos.astype(BF16).astype(np.float32), sin.astype(BF16).astype(np.float32)


def rotation(cos, sin):
    return np.stack([np.stack([cos, sin]), np.stack([-sin, cos])])


def first_table():
    turn = rotation(*small_tables(FA))
    turn = turn.reshape(2, 2, FA // 2, 2, FA)
    table = np.einsum("dchlk,ef->edklchf", turn, np.eye(2))
    return table.reshape(4 * FA, 4 * FA).astype(BF16)


def second_table(length, stations, cores=None):
    turn = rotation(*small_tables(length)) * (FA * length) ** -0.5
    turn = turn.reshape(2, 2, length, stations, cores or 1, -1)
    order = "nsdqmctb" if cores is None else "nqdsmctb"
    table = np.einsum("dcbnqm,st->" + order, turn, np.eye(2))
    return table.reshape(4 * length, 4 * length).astype(BF16)


def twist_tables(length):
    cos, sin = cos_sin(np.outer(np.arange(FA), np.arange(length)), FA * length)
    return np.stack([np.tile(cos, (1, 2)), np.tile(sin, (1, 2))]).astype(np.float32)


def rows_dot(left, right, axis):
    return lax.dot_general(left, right, (((1,), (axis,)), ((), ())), preferred_element_type=F32)


def spectra_kernel(first, count, taps, stations, last, split, *refs):
    samples, earlier, passed, prototype, first_hbm, twist_hbm, second_hbm = refs[:7]
    outs = refs[7 : 7 + stations]
    refs = refs[7 + stations :]
    tail = None
    if last or split:
        tail, refs = refs[0], refs[1:]
    frames, wide, filtered, proto, weights, first_ref, twist_ref, second_in, second, sems = refs
    per = FA
    held = (taps - 1) * per
    total = held + count * per
    tables = [
        pltpu.make_async_copy(source, target, sems.at[at])
        for at, (source, target) in enumerate(
            ((first_hbm, first_ref), (twist_hbm, twist_ref), (second_hbm, second_in))
        )
    ]
    proto_copy = pltpu.make_async_copy(prototype, proto, sems.at[3])
    proto_copy.start()
    lead = 0 if first >= taps - 1 else held
    copies = [
        pltpu.make_async_copy(
            samples.at[comp, pl.ds(first * per - held + lead, total - lead)],
            frames.at[comp, pl.ds(lead, total - lead)],
            sems.at[4 + comp],
        )
        for comp in range(2)
    ]
    for copy in copies + tables:
        copy.start()
    if lead:
        chan = lax.axis_index("chan")
        history = frames.at[:, pl.ds(0, held)]

        @pl.when(chan == 0)
        def _():
            pltpu.make_async_copy(earlier, history, sems.at[6]).start()

        @pl.when(chan != 0)
        def _():
            pltpu.make_async_copy(passed, history, sems.at[6]).start()

        copies.append(pltpu.make_async_copy(earlier, history, sems.at[6]))
    proto_copy.wait()
    for high in range(per // 2):
        for group in range(taps // 8):
            lane = high * LANES
            rows = proto[group * 8 : (group + 1) * 8, lane : lane + LANES]
            for member in range(2):
                at = group * 8 * per + 2 * high + member
                weights[pl.ds(at, 8, stride=per)] = rows
    for copy in copies:
        copy.wait()
    if last:
        tail_copy = pltpu.make_async_copy(
            frames.at[:, pl.ds(count * per, held)], tail, sems.at[6]
        )
        tail_copy.start()

    def widen(start, rows):
        for comp in range(2):
            wide[comp, pl.ds(start, rows)] = frames[comp, pl.ds(start, rows)].astype(F32)

    rows = 5 * per

    def widen_rows(index, carry):
        widen(pl.multiple_of(index * rows, per), rows)
        return carry

    lax.fori_loop(0, total // rows, widen_rows, 0)
    if total % rows:
        widen(total - total % rows, total % rows)

    def strip(index, carry):
        comp = index // (per // 16)
        row = (index % (per // 16)) * 16

        def run(block, carry):
            window = []
            for step in range(taps - 1 + STEP):
                at = pl.multiple_of((block * STEP + step) * per + row, 16)
                window.append(wide[comp, pl.ds(at, 16)])
            sums = None
            for tap in range(taps):
                weight = weights[pl.ds(pl.multiple_of(tap * per + row, 16), 16)]
                terms = [weight * window[tap + step] for step in range(STEP)]
                sums = terms if sums is None else [x + y for x, y in zip(sums, terms)]
            for step in range(STEP):
                at = pl.multiple_of(comp * per + row, 16)
                filtered[block * STEP + step, pl.ds(at, 16)] = sums[step].astype(BF16)
            return carry

        return lax.fori_loop(0, count // STEP, run, carry)

    lax.fori_loop(0, 2 * per // 16, strip, 0)
    for copy in tables:
        copy.wait()
    share = second_in.shape[0] // stations
    me = lax.axis_index("stn")
    parts = 2 if split else 1
    block = share // parts
    for part in range(parts):
        core = (lax.axis_index("chan") ^ part) * block if split else 0
        for offset in range(stations):
            start = pl.multiple_of((me ^ offset) * share + core, block)
            at = (part * stations + offset) * block
            second[at : at + block] = second_in[pl.ds(start, block)]
    low_half = lax.broadcasted_iota(jnp.int32, (2 * per, LANES), 1) < LANES // 2

    def transform(index, carry):
        mixed = []
        for pair in range(2):
            even = filtered[index * 4 + 2 * pair].astype(F32)
            odd = filtered[index * 4 + 2 * pair + 1].astype(F32)
            low = jnp.where(low_half, even, pltpu.roll(odd, LANES // 2, 1))
            high = jnp.where(low_half, pltpu.roll(even, LANES // 2, 1), odd)
            mixed.append(jnp.concatenate([low.astype(BF16), high.astype(BF16)], axis=0))
        g = rows_dot(first_ref[...], jnp.concatenate(mixed, axis=1), 0)
        cos, sin = twist_ref[0], twist_ref[1]
        inner = []
        for member in range(2):
            for pair in range(2):
                lane = pair * LANES
                g_re = g[2 * member * FA : (2 * member + 1) * FA, lane : lane + LANES]
                g_im = g[(2 * member + 1) * FA : (2 * member + 2) * FA, lane : lane + LANES]
                inner_re = (g_re * cos + g_im * sin).astype(BF16)
                inner_im = (g_im * cos - g_re * sin).astype(BF16)
                inner.append(jnp.concatenate([inner_re, inner_im], axis=1))
        spectra = rows_dot(second[...], jnp.concatenate(inner, axis=0), 1).astype(BF16)
        for member in range(2):
            lane = member * LANES
            for offset in range(stations):
                row = offset * block
                outs[offset][index, member] = spectra[row : row + block, lane : lane + LANES]
                if split:
                    row = (stations + offset) * block
                    tail[offset, index, member] = spectra[row : row + block, lane : lane + LANES]
        return carry

    lax.fori_loop(0, count // 4, transform, 0, unroll=5 if count % 40 == 0 else 2 if count % 16 else 8 if count % 32 == 0 else 4)
    if last:
        tail_copy.wait()


def spectra_of(first, count, samples, earlier, passed, prototype, stations, last, cores=None):
    taps, channels = prototype.shape
    length = channels // FA
    share = 4 * length // stations
    held = (taps - 1) * FA
    rows = held + count * FA
    tables = (first_table(), twist_tables(length), second_table(length, stations, cores))
    sent = (count // 4, 2, share // (cores or 1), LANES)
    out_shape = [jax.ShapeDtypeStruct(sent, BF16)] * stations
    if cores:
        out_shape.append(jax.ShapeDtypeStruct((stations,) + sent, BF16))
    if last:
        out_shape.append(jax.ShapeDtypeStruct((2, held, LANES), BF16))
    return pl.pallas_call(
        functools.partial(spectra_kernel, first, count, taps, stations, last, bool(cores)),
        out_shape=out_shape,
        in_specs=[ANY] * 7,
        out_specs=[VMEM] * stations + [ANY] * last + [VMEM] * bool(cores),
        scratch_shapes=[
            pltpu.VMEM((2, rows, LANES), BF16),
            pltpu.VMEM((2, rows, LANES), F32),
            pltpu.VMEM((count, 2 * FA, LANES), BF16),
            pltpu.VMEM((taps, channels), F32),
            pltpu.VMEM((taps * FA, LANES), F32),
            pltpu.VMEM((4 * FA, 4 * FA), BF16),
            pltpu.VMEM((2, FA, LANES), F32),
            pltpu.VMEM((4 * length, 4 * length), BF16),
            pltpu.VMEM((4 * length, 4 * length), BF16),
            pltpu.SemaphoreType.DMA((7,)),
        ],
        cost_estimate=pl.CostEstimate(
            flops=count * 8 * 10**6, bytes_accessed=count * 65536, transcendentals=0
        ),
        compiler_params=pltpu.CompilerParams(vmem_limit_bytes=(58 if last else 20) * 2**20),
    )(samples, earlier, passed, prototype, *tables)


def join_kernel(stations, *refs):
    mine, twin, outs = refs[:stations], refs[stations], refs[stations + 1 :]
    half = mine[0].shape[0]
    for offset in range(stations):
        outs[offset][:half] = mine[offset][...]
        outs[offset][half:] = twin[offset]


def join(mine, twin):
    shape = (2 * mine[0].shape[0],) + mine[0].shape[1:]
    return pl.pallas_call(
        functools.partial(join_kernel, len(mine)),
        out_shape=[jax.ShapeDtypeStruct(shape, BF16)] * len(mine),
        in_specs=[VMEM] * (len(mine) + 1),
        out_specs=[VMEM] * len(mine),
        compiler_params=pltpu.CompilerParams(vmem_limit_bytes=12 * 2**20),
        cost_estimate=pl.CostEstimate(flops=10**6, bytes_accessed=10**6, transcendentals=0),
        name="join",
    )(*mine, twin)


def pair_rows(inputs):
    pairs = [(a, b) for a in range(inputs) for b in range(a, inputs)]
    return {pair: row for row, pair in enumerate(pairs)}


def products_kernel(inputs, carried, part, *refs):
    before = refs[-2] if carried else None
    blocks = refs[: -2 if carried else -1]
    out = refs[-1]
    rows = pair_rows(inputs)
    span = SUBLANES
    group = 4
    last = inputs - group

    def load(member, step, low):
        tile = blocks[member // 2][step, member % 2, low * 2 * span : (low + 1) * 2 * span]
        both = tile.astype(F32)
        return both[:span], both[span:]

    for left in range(0, inputs, group):
        for right in range(left, inputs, group):
            a_list = range(left, left + group)
            b_list = range(right, right + group)
            members = [(a, b) for a in a_list for b in b_list if a <= b]
            wanted = [(a, b, comp) for a, b in members for comp in range(2) if a != b or comp == 0]
            active = part == "all" or (part == "early") == (right < last)
            known = carried and (part != "late" or right < last or carried == 2)
            if not (active or known):
                continue

            def body(step, sums):
                for low in range(blocks[0].shape[2] // (2 * span)):
                    a_side = {a: load(a, step, low) for a in a_list}
                    b_side = a_side
                    if right != left:
                        b_side = {b: load(b, step, low) for b in b_list}
                    new = []
                    for total, (a, b, comp) in zip(sums, wanted):
                        a_re, a_im = a_side[a]
                        b_re, b_im = b_side[b]
                        if comp == 0:
                            new.append(total + a_re * b_re + a_im * b_im)
                        else:
                            new.append(total + a_im * b_re - a_re * b_im)
                    sums = new
                return sums

            sums = []
            for a, b, comp in wanted:
                at = (2 * rows[a, b] + comp) * span
                sums.append(before[at : at + span] if known else jnp.zeros((span, LANES), F32))
            if active:
                sums = lax.fori_loop(0, blocks[0].shape[0], body, sums, unroll=2)
            sums = dict(zip(wanted, sums))
            for a, b in members:
                re = sums[a, b, 0]
                im = sums.get((a, b, 1), jnp.zeros_like(re))
                at = rows[a, b] * span
                if part == "late":
                    low_half = lax.broadcasted_iota(jnp.int32, re.shape, 1) < LANES // 2
                    re = re + pltpu.roll(re, LANES // 2, 1)
                    im = im + pltpu.roll(im, LANES // 2, 1)
                    out[at : at + span] = jnp.where(low_half, re, im)
                else:
                    out[2 * at : 2 * at + span] = re
                    out[2 * at + span : 2 * at + 2 * span] = im


def products_of(blocks, before, part="all", whole=True):
    inputs = 2 * len(blocks)
    count = len(pair_rows(inputs)) * (1 if part == "late" else 2)
    carried = 0 if before is None else 1 + whole
    used = blocks[:-2] if part == "early" else blocks
    arrays = list(used) + ([before] if carried else [])
    steps = blocks[0].shape[0] * blocks[0].shape[2] // 8
    return pl.pallas_call(
        functools.partial(products_kernel, inputs, carried, part),
        out_shape=jax.ShapeDtypeStruct((count * SUBLANES, LANES), F32),
        in_specs=[VMEM] * len(arrays),
        out_specs=VMEM,
        compiler_params=pltpu.CompilerParams(vmem_limit_bytes=12 * 2**20),
        cost_estimate=pl.CostEstimate(
            flops=steps * 4 * 10**6, bytes_accessed=steps * 65536, transcendentals=0
        ),
    )(*arrays)


def visibility_kernel(stations, total, own, other, late, out):
    inputs = 2 * stations
    rows = pair_rows(inputs)
    count = len(rows)
    span = own.shape[0] // count
    mine = span // 2
    width = inputs * inputs
    turn = 2 * lax.axis_index("stn")
    row = lax.broadcasted_iota(jnp.int32, (count, width), 0)
    col = lax.broadcasted_iota(jnp.int32, (count, width), 1)
    i_rel = jnp.zeros_like(row)
    for a in range(1, inputs):
        i_rel = i_rel + (row >= rows[a, a]).astype(jnp.int32)
    j_rel = row - (i_rel * inputs - i_rel * (i_rel - 1) // 2) + i_rel
    i_at, j_at = i_rel ^ turn, j_rel ^ turn
    plain = col == i_at * inputs + j_at
    mirror = col == j_at * inputs + i_at
    picks = [
        jnp.where(plain, 1.0, jnp.where(mirror, sign, 0.0)).astype(BF16) for sign in (1.0, -1.0)
    ]
    core = lax.axis_index("chan")
    for low in range(mine):
        at = pl.ds(core * mine + low, count, stride=span)
        both = own[at] + other[at]
        for half in range(2):
            both = both + late[pl.ds(half * mine + low, count, stride=span)]
        lanes = (both * (1.0 / total)).T
        for comp in range(2):
            rest = lanes[comp * FA : (comp + 1) * FA]
            value = None
            for _ in range(3):
                piece = rest.astype(BF16)
                part = rows_dot(piece, picks[comp], 0)
                value = part if value is None else value + part
                rest = rest - piece.astype(F32)
            out[comp, low * FA : (low + 1) * FA] = value


def send_order(stations):
    return sorted(range(1, stations), key=lambda d: (d < stations // 2, d))


def shards(voltage, earlier_samples, prototype):
    components, local_inputs, samples = voltage.shape
    _, channels = prototype.shape
    spectra_here = samples // channels
    length = channels // FA
    stations = lax.axis_size("stn")
    cores = lax.axis_size("chan")
    total = spectra_here * cores

    def by_tile(block):
        tiles = block.reshape(components, local_inputs, -1, LANES)
        return jnp.transpose(tiles, (0, 2, 1, 3)).reshape(components, -1, LANES)

    stream = by_tile(voltage)
    earlier = by_tile(earlier_samples)
    whole = sum(SHARES)
    staged = length // stations == SUBLANES
    first = spectra_here
    chunks = []
    passed = earlier
    for chunk, share in enumerate(SHARES):
        count = spectra_here * share // whole
        first -= count
        history = earlier if first else passed
        blocks = list(
            spectra_of(
                first,
                count,
                stream,
                earlier,
                history,
                prototype,
                stations,
                chunk == 0,
                cores if staged and first == 0 else None,
            )
        )
        if chunk == 0:
            route = [(i, i + 1) for i in range(cores - 1)]
            passed = lax.ppermute(blocks.pop(), "chan", route)
        chunks.append(blocks)
    if staged:
        swap = [(i, i ^ 1) for i in range(cores)]
        sums = None
        for chunk, blocks in enumerate(chunks):
            late = chunk == len(chunks) - 1
            if late:
                twin = lax.ppermute(blocks.pop(), "chan", swap)
                blocks = list(join(blocks, twin))
            for offset in send_order(stations):
                route = [(i, i ^ offset) for i in range(stations)]
                blocks[offset] = lax.ppermute(blocks[offset], "stn", route)
            if chunk < len(chunks) - 2:
                sums = products_of(blocks, sums)
                continue
            start = None if late else sums
            early = products_of(blocks, start, "early")
            newest = products_of(blocks, early, "late", not late)
            if not late:
                sums = newest
        other = lax.ppermute(sums, "chan", swap)
        owned = channels // (stations * cores)
        return pl.pallas_call(
            functools.partial(visibility_kernel, stations, total),
            out_shape=jax.ShapeDtypeStruct((2, owned, 4 * stations * stations), F32),
            in_specs=[VMEM] * 3,
            out_specs=VMEM,
            compiler_params=pltpu.CompilerParams(vmem_limit_bytes=12 * 2**20),
            name="visibility",
        )(sums, other, newest)
    joined = [jnp.concatenate([blocks[d] for blocks in chunks]) for d in range(stations)]
    joined = jnp.stack(joined)[jnp.arange(stations) ^ lax.axis_index("stn")]
    span = length // stations // cores
    joined = joined.reshape(stations, spectra_here // 4, 2, 2, 2, cores, span, 2, FA)
    joined = jnp.transpose(joined, (4, 2, 1, 7, 3, 0, 5, 6, 8))
    joined = joined.reshape(2, 2, spectra_here, stations * cores, span * FA)
    moved = lax.all_to_all(joined, ("stn", "chan"), split_axis=3, concat_axis=3, tiled=True)
    moved = moved.reshape(2, 2, spectra_here, stations, cores, span * FA)
    moved = jnp.transpose(moved, (0, 3, 1, 4, 2, 5))
    moved = moved.reshape(2, 2 * stations, total, span * FA)
    products = jnp.einsum("xisc,yjsc->xycij", moved, moved, preferred_element_type=F32)
    real_sum = products[0, 0] + products[1, 1]
    imag_sum = products[1, 0] - products[0, 1]
    averaged = jnp.stack([real_sum, imag_sum]) / total
    return averaged.reshape(2, span * FA, 4 * stations * stations)


def solution(mesh):
    in_specs = (P(None, ("grp", "stn"), "chan"), P(None, ("grp", "stn"), None), P())
    out_specs = P(None, ("grp", "stn", "chan"), None)

    return jax.shard_map(shards, mesh=mesh, in_specs=in_specs, out_specs=out_specs, check_vma=False)
```
